32 devices in a mesh: tm: 4 (over y, x), beam: 8 (over z, core).
Axes of the slice: x: 2, y: 2, z: 4, core: 2. Of those that a mesh axis runs over, the one named last changes fastest.
Arguments:
- element_signals: bfloat16 [2, 2048, 4096], P(None, None, ('tm', 'beam')), may hold values from -6 to 6
- beam_weights: bfloat16 [2, 1024, 2048], P(None, ('tm', 'beam')), may hold values from -0.09375 to 0.09375
- beam_order: int32 [1024], replicated, may hold values from 0 to 1023, as said below
- neighbours: int32 [1024, 6], replicated, may hold values from 0 to 1024, as said below
- leakage: bfloat16 [2, 1024, 6], replicated, may hold values from -1.5 to 1.5
- noise_var: float32 [1024], replicated, may hold values from 0.5 to 2
- bit_labels: int32 [16], replicated, may hold values from 0 to 15, each once
Outputs:
- llr: bfloat16 [4, 1024, 4096], P(None, 'beam', 'tm')
The draws below stay inside these ranges and needn't reach their ends.
Inputs may be any that keep to these rules, and one draw needn't show every extreme that they name: `beam_order`: A permutation of the 1024 beams. Position p lies in row p // 16 and column p % 16 of a hexagonal grid of 64 rows in which odd rows sit half a cell to the right. `neighbours`: row b lists the beams in the grid cells adjacent to beam b's cell (up to six, each once) and 1024 in the remaining slots. `bit_labels`: each label once.
All inputs are finite; a program needn't handle non-finite values.
Results may differ from the reference program's by a relative error of at most 0.0063.
Values may be sent and summed in bfloat16 or wider, within the bound.
No kernel may reach another device: no remote copies, remote signals or barrier semaphores. Data moves between devices by JAX's collectives and lax.ppermute only.
A program may use at most 128 MiB of HBM per device.

```python
import math
import jax
import jax.numpy as jnp
from jax import lax

E = 2048
B = 1024
COLS = 16
NBR = 6
POINTS = 16
NSAMP = 4096
N_TM = 4


def hex_layout(key):
    count = B
    order = jax.random.permutation(jax.random.fold_in(key, 11), count).astype(jnp.int32)
    position = jnp.arange(count, dtype=jnp.int32)
    row = position // COLS
    column = position % COLS
    odd_row = row % 2
    rows_total = count // COLS
    entries = []
    for row_step, column_step, tilt in ((0, -1, 0), (0, 1, 0), (-1, -1, 1), (-1, 0, 1), (1, -1, 1), (1, 0, 1)):
        new_row = row + row_step
        new_column = column + column_step + tilt * odd_row
        valid = (new_row >= 0) & (new_row < rows_total) & (new_column >= 0) & (new_column < COLS)
        target = jnp.clip(new_row * COLS + new_column, 0, count - 1)
        entries.append(jnp.where(valid, jnp.take(order, target), count))
    by_position = jnp.stack(entries, axis=1).astype(jnp.int32)
    table = jnp.zeros((count, NBR), jnp.int32).at[order].set(by_position)
    return (order, table)


def draw_beam_order(key, part):
    return hex_layout(key)[0]


def draw_neighbours(key, part):
    return hex_layout(key)[1]


def steps_of(key, dims, split, least, largest):
    loudness = 1.0
    for dim, shards_of in split:
        steps = jax.random.uniform(jax.random.fold_in(jax.random.fold_in(key, 6), dim), (shards_of,), jnp.float32, least / len(split), largest / len(split))
        loudness = loudness * jnp.repeat(jnp.exp(steps), dims[dim] // shards_of).reshape((-1,) + (1,) * (len(dims) - 1 - dim))
    return loudness


def bell_draw(rng, shape, scale, limit, shards=(), kind=jnp.bfloat16):
    loudness = steps_of(rng, shape, shards, -0.22, 0.18) if shards else 1.0
    values = jax.random.normal(rng, shape, jnp.float32) * scale * loudness
    return jnp.minimum(jnp.maximum(values, -limit), limit).astype(kind)


def setup_inputs(seed: int = 0) -> dict:
    arg_keys = jax.random.split(jax.random.key(seed), 8)
    return {
        "element_signals": bell_draw(arg_keys[0], (2, E, NSAMP), 1.0, 6.0, ((2, 32),)),
        "beam_weights": bell_draw(arg_keys[1], (2, B, E), (2 * E) ** -0.5, 0.09375, ((1, 32),)),
        "beam_order": draw_beam_order(jax.random.fold_in(arg_keys[7], 71), 0),
        "neighbours": draw_neighbours(jax.random.fold_in(arg_keys[7], 71), 0),
        "leakage": bell_draw(arg_keys[4], (2, B, NBR), 0.25, 1.5),
        "noise_var": jnp.clip(jnp.exp(jax.random.uniform(arg_keys[5], (B,), jnp.float32, math.log(0.5), math.log(2.0))), 0.5, 2.0),
        "bit_labels": jax.random.permutation(arg_keys[6], POINTS).astype(jnp.int32),
    }


LEVEL = 0.31622776601683794
HUGE = 1.0e30


def label_flags(bit_labels):
    return [[(bit_labels[point] // (2 ** bit)) % 2 == 1 for bit in range(4)] for point in range(16)]


def point_value(point):
    return ((2 * (point // 4) - 3) * LEVEL, (2 * (point % 4) - 3) * LEVEL)


def bit_metrics(field_real, field_imaginary, variance, flags):
    lowest_one = [jnp.full(field_real.shape, HUGE, jnp.float32) for bit in range(4)]
    lowest_zero = [jnp.full(field_real.shape, HUGE, jnp.float32) for bit in range(4)]
    for point in range(16):
        real_value, imaginary_value = point_value(point)
        distance = (field_real - real_value) ** 2 + (field_imaginary - imaginary_value) ** 2
        for bit in range(4):
            flag = flags[point][bit]
            lowest_one[bit] = jnp.where(flag, jnp.minimum(lowest_one[bit], distance), lowest_one[bit])
            lowest_zero[bit] = jnp.where(flag, lowest_zero[bit], jnp.minimum(lowest_zero[bit], distance))
    return [(lowest_one[bit] - lowest_zero[bit]) / variance for bit in range(4)]


def soft_symbols(field_real, field_imaginary, variance, flags):
    metrics = bit_metrics(field_real, field_imaginary, variance, flags)
    chance = [jax.nn.sigmoid(metric) for metric in metrics]
    total_real = jnp.zeros(field_real.shape, jnp.float32)
    total_imaginary = jnp.zeros(field_real.shape, jnp.float32)
    for point in range(16):
        real_value, imaginary_value = point_value(point)
        weight = jnp.ones(field_real.shape, jnp.float32)
        for bit in range(4):
            weight = weight * jnp.where(flags[point][bit], 1.0 - chance[bit], chance[bit])
        total_real = total_real + real_value * weight
        total_imaginary = total_imaginary + imaginary_value * weight
    return jnp.stack([total_real, total_imaginary]).astype(jnp.bfloat16)


def interference(soft, weights_near, near_position):
    values = soft.astype(jnp.float32)
    total_real = jnp.zeros(values.shape[1:], jnp.float32)
    total_imaginary = jnp.zeros(values.shape[1:], jnp.float32)
    for slot in range(near_position.shape[1]):
        taken = jnp.take(values, near_position[:, slot], axis=1)
        weight_real = weights_near[0][:, slot][:, None]
        weight_imaginary = weights_near[1][:, slot][:, None]
        total_real = total_real + weight_real * taken[0] - weight_imaginary * taken[1]
        total_imaginary = total_imaginary + weight_real * taken[1] + weight_imaginary * taken[0]
    return total_real, total_imaginary


def reference(element_signals, beam_weights, beam_order, neighbours, leakage, noise_var, bit_labels):
    count_beams = beam_order.shape[0]
    flags = label_flags(bit_labels)
    position_of = jnp.zeros((count_beams,), jnp.int32).at[beam_order].set(jnp.arange(count_beams, dtype=jnp.int32))
    near = jnp.take(neighbours, beam_order, axis=0)
    present = (near < count_beams).astype(jnp.float32)
    near_position = jnp.take(position_of, jnp.clip(near, 0, count_beams - 1))
    weights_near = jnp.take(leakage, beam_order, axis=1).astype(jnp.float32) * present[None]
    variance = jnp.take(noise_var, beam_order)[:, None]
    elements = element_signals.shape[1]
    total = element_signals.shape[2]
    width = total // N_TM
    blocks = jnp.transpose(element_signals.reshape(2, elements, N_TM, width), (2, 0, 1, 3))

    def one_block(signals):
        real_part = jnp.dot(beam_weights[0], signals[0], preferred_element_type=jnp.float32) - jnp.dot(beam_weights[1], signals[1], preferred_element_type=jnp.float32)
        imaginary_part = jnp.dot(beam_weights[0], signals[1], preferred_element_type=jnp.float32) + jnp.dot(beam_weights[1], signals[0], preferred_element_type=jnp.float32)
        beams = jnp.stack([real_part, imaginary_part]).astype(jnp.bfloat16)
        ordered = jnp.take(beams, beam_order, axis=1)
        base_real = ordered[0].astype(jnp.float32)
        base_imaginary = ordered[1].astype(jnp.float32)
        field_real = base_real
        field_imaginary = base_imaginary
        for section in range(2):
            soft = soft_symbols(field_real, field_imaginary, variance, flags)
            cross_real, cross_imaginary = interference(soft, weights_near, near_position)
            field_real = base_real - cross_real
            field_imaginary = base_imaginary - cross_imaginary
        return jnp.stack(bit_metrics(field_real, field_imaginary, variance, flags)).astype(jnp.bfloat16)

    result = lax.map(one_block, blocks)
    return jnp.transpose(result, (1, 2, 0, 3)).reshape(result.shape[1], count_beams, total)
```

```python
import functools

import jax
import jax.numpy as jnp
import numpy as np
from jax import lax
from jax.experimental import pallas as pl
from jax.experimental.pallas import tpu as pltpu
from jax.sharding import PartitionSpec as P

COLS = 16
HALO = 2 * COLS
LEVEL = 0.31622776601683794
LANES = 128
MEBI = 1 << 20


def beams_kernel(pieces, groups, steps, *refs):
    weights = refs[:pieces]
    signals = refs[pieces : pieces + groups]
    outs = refs[pieces + groups : pieces + 2 * groups]
    total = refs[-1]
    step = pl.program_id(0)

    @pl.when(step == 0)
    def _():
        total[...] = jnp.zeros_like(total)

    w_real = jnp.concatenate([w[0] for w in weights], axis=0)
    w_imag = jnp.concatenate([w[1] for w in weights], axis=0)
    x_real = jnp.concatenate([x[0] for x in signals], axis=1)
    x_imag = jnp.concatenate([x[1] for x in signals], axis=1)
    dot = functools.partial(jnp.dot, preferred_element_type=jnp.float32)
    total[0] += dot(w_real, x_real) - dot(w_imag, x_imag)
    total[1] += dot(w_real, x_imag) + dot(w_imag, x_real)

    @pl.when(step == steps - 1)
    def _():
        for g in range(groups):
            outs[g][...] = total[:, :, g * LANES : (g + 1) * LANES].astype(jnp.bfloat16)


def form_beams(weights, signals):
    pieces, groups = len(weights), len(signals)
    rows, elements = weights[0].shape[1:]
    samples = signals[0].shape[2]
    depth = min(512, elements)
    steps = elements // depth
    all_rows = pieces * rows
    return pl.pallas_call(
        functools.partial(beams_kernel, pieces, groups, steps),
        grid=(steps,),
        in_specs=[pl.BlockSpec((2, rows, depth), lambda k: (0, 0, k))] * pieces
        + [pl.BlockSpec((2, depth, samples), lambda k: (0, k, 0))] * groups,
        out_specs=[pl.BlockSpec((2, all_rows, samples), lambda k: (0, 0, 0))] * groups,
        out_shape=[jax.ShapeDtypeStruct((2, all_rows, samples), jnp.bfloat16)] * groups,
        scratch_shapes=[pltpu.VMEM((2, all_rows, groups * samples), jnp.float32)],
        compiler_params=pltpu.CompilerParams(vmem_limit_bytes=40 * MEBI),
        cost_estimate=pl.CostEstimate(
            flops=8 * all_rows * elements * groups * samples,
            bytes_accessed=4 * elements * (all_rows + groups * samples),
            transcendentals=0,
        ),
        name="form_beams",
    )(*weights, *signals)


def order_kernel(parts, *refs):
    select, beams, out = refs[0], refs[1 : 1 + parts], refs[-1]
    real = jnp.concatenate([b[0] for b in beams], axis=0)
    imag = jnp.concatenate([b[1] for b in beams], axis=0)
    both = jnp.concatenate([real, imag], axis=1)
    picked = jnp.dot(select[0], both, preferred_element_type=jnp.float32).astype(jnp.bfloat16)
    samples = real.shape[1]
    out[0, 0] = picked[:, :samples]
    out[0, 1] = picked[:, samples:]


def order_beams(select, beams):
    tiles, rows, count = select.shape
    part_rows, samples = beams[0].shape[1:]
    return pl.pallas_call(
        functools.partial(order_kernel, len(beams)),
        grid=(tiles,),
        in_specs=[pl.BlockSpec((1, rows, count), lambda d: (d, 0, 0))]
        + [pl.BlockSpec((2, part_rows, samples), lambda d: (0, 0, 0))] * len(beams),
        out_specs=pl.BlockSpec((1, 2, rows, samples), lambda d: (d, 0, 0, 0)),
        out_shape=jax.ShapeDtypeStruct((tiles, 2, rows, samples), jnp.bfloat16),
        compiler_params=pltpu.CompilerParams(vmem_limit_bytes=40 * MEBI),
        cost_estimate=pl.CostEstimate(
            flops=4 * tiles * rows * count * samples,
            bytes_accessed=2 * tiles * rows * (count + 2 * samples),
            transcendentals=0,
        ),
        name="order_beams",
    )(select, *beams)


def bit_gaps(real, imag, index, scratch):
    shift = 8.0 * LEVEL * LEVEL
    for axis, field in ((0, real), (1, imag)):
        step = field * (2.0 * LEVEL)
        triple = field * (6.0 * LEVEL)
        scratch[axis * 4] = shift + triple
        scratch[axis * 4 + 1] = step
        scratch[axis * 4 + 2] = -step
        scratch[axis * 4 + 3] = shift - triple
    far = [scratch[index[label]] + scratch[index[16 + label]] for label in range(16)]
    least = jnp.minimum
    low = [
        least(least(far[b], far[b + 4]), least(far[b + 8], far[b + 12])) for b in range(4)
    ]
    high = [
        least(least(far[4 * b], far[4 * b + 1]), least(far[4 * b + 2], far[4 * b + 3]))
        for b in range(4)
    ]
    gaps = []
    for part in (low, high):
        gaps.append(least(part[1], part[3]) - least(part[0], part[2]))
        gaps.append(least(part[2], part[3]) - least(part[0], part[1]))
    return gaps


def expand(signs, coefs, base):
    terms = [coefs[base + t] + signs[3] * coefs[base + t + 8] for t in range(8)]
    terms = [terms[t] + signs[2] * terms[t + 4] for t in range(4)]
    terms = [terms[t] + signs[1] * terms[t + 2] for t in range(2)]
    return terms[0] + signs[0] * terms[1]


def soft_kernel(shape, index, field, first, second, scale, coefs, out, s_one, s_two, rest, scratch):
    blocks, rows, inner, tile = shape
    margin = (rows - inner) // 2
    dot = functools.partial(jnp.dot, preferred_element_type=jnp.float32)
    chunk = 16

    def tiles(value):
        return value.reshape(chunk // 8, 8, LANES)

    def soften(real, imag, start, slot):
        gaps = bit_gaps(real, imag, index, scratch.at[slot])
        half = tiles(scale[pl.ds(start, chunk), :])
        signs = [jnp.tanh(gap * half) for gap in gaps]
        return [
            expand(signs, coefs, base).reshape(chunk, LANES).astype(jnp.bfloat16)
            for base in (0, 16)
        ]

    count = 0
    for block in range(blocks):
        lanes = pl.ds(block * LANES, LANES)
        for start in range(0, rows, chunk):
            real = tiles(field[block, 0, start : start + chunk, :].astype(jnp.float32))
            imag = tiles(field[block, 1, start : start + chunk, :].astype(jnp.float32))
            a, b = soften(real, imag, start, count % 2)
            s_one[start : start + chunk, lanes] = a
            s_one[rows + start : rows + start + chunk, lanes] = b
            count += 1
    rest[...] = dot(first[...], s_one[...])
    for block in range(blocks):
        lanes = pl.ds(block * LANES, LANES)
        for start in range(0, inner, chunk):
            away = start + margin
            real = field[block, 0, away : away + chunk, :].astype(jnp.float32) - rest[
                start : start + chunk, lanes
            ]
            imag = field[block, 1, away : away + chunk, :].astype(jnp.float32) - rest[
                inner + start : inner + start + chunk, lanes
            ]
            a, b = soften(tiles(real), tiles(imag), away, count % 2)
            s_two[start : start + chunk, lanes] = a
            s_two[inner + start : inner + start + chunk, lanes] = b
            count += 1
    rest[0 : 2 * tile, :] = dot(second[...], s_two[...])
    for block in range(blocks):
        lanes = pl.ds(block * LANES, LANES)
        for start in range(0, tile, chunk):
            away = start + 2 * margin
            real = field[block, 0, away : away + chunk, :].astype(jnp.float32) - rest[
                start : start + chunk, lanes
            ]
            imag = field[block, 1, away : away + chunk, :].astype(jnp.float32) - rest[
                tile + start : tile + start + chunk, lanes
            ]
            gaps = bit_gaps(tiles(real), tiles(imag), index, scratch.at[count % 2])
            whole = 2.0 * tiles(scale[away : away + chunk, :])
            for bit in range(4):
                out[bit, start : start + chunk, lanes] = (
                    (gaps[bit] * whole).reshape(chunk, LANES).astype(jnp.bfloat16)
                )
            count += 1


def cancel(index, field, first, second, scale, coefs):
    sources, _, rows, samples = field.shape
    inner, tile = first.shape[0] // 2, second.shape[0] // 2
    blocks = 2
    wide = blocks * samples
    elements = sources * samples
    return pl.pallas_call(
        functools.partial(soft_kernel, (blocks, rows, inner, tile)),
        grid=(sources // blocks,),
        in_specs=[
            pl.BlockSpec(memory_space=pltpu.SMEM),
            pl.BlockSpec((blocks, 2, rows, samples), lambda s: (s, 0, 0, 0)),
            pl.BlockSpec(first.shape, lambda s: (0, 0)),
            pl.BlockSpec(second.shape, lambda s: (0, 0)),
            pl.BlockSpec(scale.shape, lambda s: (0, 0)),
            pl.BlockSpec(coefs.shape, lambda s: (0, 0, 0)),
        ],
        out_specs=pl.BlockSpec((4, tile, wide), lambda s: (0, 0, s)),
        out_shape=jax.ShapeDtypeStruct((4, tile, elements), jnp.bfloat16),
        scratch_shapes=[
            pltpu.VMEM((2 * rows, wide), jnp.bfloat16),
            pltpu.VMEM((2 * inner, wide), jnp.bfloat16),
            pltpu.VMEM((2 * inner, wide), jnp.float32),
            pltpu.VMEM((2, 8, 2, 8, LANES), jnp.float32),
        ],
        compiler_params=pltpu.CompilerParams(vmem_limit_bytes=40 * MEBI),
        cost_estimate=pl.CostEstimate(
            flops=130 * (rows + inner + tile) * elements,
            bytes_accessed=4 * rows * elements + 8 * tile * elements,
            transcendentals=4 * (rows + inner) * elements,
        ),
        name="cancel",
    )(index, field, first, second, scale, coefs)


class Places:
    def __init__(self, mesh):
        self.tm, self.beam = mesh.shape["tm"], mesh.shape["beam"]
        self.ny, self.nz = self.tm // 2, self.beam // 2

    def flat(self, y, x, z, core):
        return (y * 2 + x) * self.beam + z * 2 + core

    def permute(self, value, move):
        pairs = []
        for y in range(self.ny):
            for x in range(2):
                for z in range(self.nz):
                    for core in range(2):
                        pairs.append(
                            (self.flat(y, x, z, core), self.flat(*move(y, x, z, core)))
                        )
        return lax.ppermute(value, ("tm", "beam"), pairs)

    def across_core(self, value):
        return self.permute(value, lambda y, x, z, core: (y, x, z, 1 - core))

    def across_x(self, value):
        return self.permute(value, lambda y, x, z, core: (y, 1 - x, z, core))

    def across_y(self, value):
        return self.permute(value, lambda y, x, z, core: (1 - y, x, z, core))

    def along_z(self, value, k):
        return self.permute(value, lambda y, x, z, core: (y, x, (z + k) % self.nz, core))


def all_beams(places, element_signals, beam_weights):
    rows = beam_weights.shape[1]
    near = jnp.arange(rows, dtype=jnp.int32)
    if places.ny != 2 or places.nz != 4:
        gathered = lax.all_gather(beam_weights, ("tm", "beam"), axis=1, tiled=True)
        beams = form_beams([gathered], [element_signals])
        return beams, jnp.arange(gathered.shape[1], dtype=jnp.int32)
    half = element_signals.shape[1] // 2
    x_parts = [
        places.across_x(element_signals[:, i * half : (i + 1) * half]) for i in range(2)
    ]
    shifts = (0, 1, 3, 2)
    column = [beam_weights] + [places.along_z(beam_weights, k) for k in shifts[1:]]
    other = [places.across_y(piece) for piece in column]
    from_core = places.across_core(element_signals)
    from_x = jnp.concatenate(x_parts, axis=1)
    from_both = jnp.concatenate([places.across_core(part) for part in x_parts], axis=1)
    made = form_beams(column + other, [element_signals, from_core, from_x, from_both])
    beams = [
        made[0],
        places.across_core(made[1]),
        places.across_x(made[2]),
        places.permute(made[3], lambda y, x, z, core: (y, 1 - x, z, 1 - core)),
    ]
    kinds = [
        (mx, mc, a, k)
        for mx, mc in ((0, 0), (0, 1), (1, 0), (1, 1))
        for a in range(2)
        for k in shifts
    ]
    mx, mc, a, k = (np.array(v, np.int32) for v in zip(*kinds))
    tm, beam = lax.axis_index("tm"), lax.axis_index("beam")
    source = places.flat(
        (tm // 2) ^ a, (tm % 2) ^ mx, (beam // 2 - k) % places.nz, (beam % 2) ^ mc
    )
    return beams, (source[:, None] * rows + near[None, :]).reshape(-1)


def constellation(bit_labels):
    points = jnp.arange(16, dtype=jnp.int32)
    holds = bit_labels[None, :] == points[:, None]
    point = jnp.sum(jnp.where(holds, points[None, :], 0), axis=1)
    index = jnp.concatenate([point // 4, 4 + point % 4])
    walsh = np.array(
        [[(-1.0) ** bin(t & m).count("1") for m in range(16)] for t in range(16)], np.float32
    )
    values = jnp.stack([point // 4, point % 4])
    values = (2 * values - 3).astype(jnp.float32) * LEVEL
    coefs = jnp.sum(values[:, None, :] * walsh[None], axis=2) / 16.0
    return index, jnp.broadcast_to(coefs.reshape(32, 1, 1), (32, 8, LANES))


def on_device(places, element_signals, beam_weights, beam_order, neighbours, leakage, noise_var, bit_labels):
    count = beam_order.shape[0]
    tile = count // places.beam
    rows = tile + 2 * HALO
    slots = neighbours.shape[1]
    starts = np.arange(places.beam)[:, None] * tile - HALO + np.arange(rows)[None, :]
    windows = jnp.where(
        (starts >= 0) & (starts < count), beam_order[np.clip(starts, 0, count - 1)], -1
    )
    mine = lax.axis_index("beam")
    own = windows[mine]
    table = jnp.concatenate(
        [
            neighbours.astype(jnp.float32),
            leakage[0].astype(jnp.float32),
            leakage[1].astype(jnp.float32),
            noise_var[:, None],
        ],
        axis=1,
    )
    taken = jnp.take(table, own, axis=0, mode="clip")
    near, noise = taken[:, :slots], taken[:, 3 * slots]
    hits = near[:, :, None] == own.astype(jnp.float32)[None, None, :]
    real, imag = (
        jnp.sum(jnp.where(hits, taken[:, i * slots : (i + 1) * slots, None], 0.0), axis=1)
        for i in (1, 2)
    )
    scale = jnp.broadcast_to(0.5 / noise[:, None], (rows, LANES))

    def crossing(out, cols):
        r, i = real[out:-out, cols : rows - cols], imag[out:-out, cols : rows - cols]
        top, bottom = jnp.concatenate([r, -i], axis=1), jnp.concatenate([i, r], axis=1)
        return jnp.concatenate([top, bottom], axis=0).astype(jnp.bfloat16)

    index, coefs = constellation(bit_labels)
    beams, held = all_beams(places, element_signals, beam_weights)
    select = (windows[:, :, None] == held[None, None, :]).astype(jnp.bfloat16)
    ordered = order_beams(select, beams)
    field = lax.all_to_all(ordered, "beam", split_axis=0, concat_axis=0, tiled=True)
    return cancel(index, field, crossing(COLS, 0), crossing(2 * COLS, COLS), scale, coefs)


def solution(mesh):
    in_specs = (
        P(None, None, ("tm", "beam")),
        P(None, ("tm", "beam"), None),
        P(),
        P(),
        P(),
        P(),
        P(),
    )
    return jax.shard_map(
        functools.partial(on_device, Places(mesh)),
        mesh=mesh,
        in_specs=in_specs,
        out_specs=P(None, "beam", "tm"),
        check_vma=False,
    )
```

```python
import functools
import math

import jax
import jax.numpy as jnp
import numpy as np
from jax import lax
from jax.experimental import pallas as pl
from jax.experimental.pallas import tpu as pltpu
from jax.sharding import PartitionSpec as P

COLS = 16
HALO = 2 * COLS
LEVEL = 0.31622776601683794
LANES = 128
MEBI = 1 << 20


def beams_kernel(pieces, *refs):
    weights, signals, out, total = refs[:pieces], *refs[pieces:]
    elements = weights[0].shape[2]
    depth = math.gcd(elements, 512)
    for start in range(0, elements, depth):
        part = slice(start, start + depth)
        stack = jnp.concatenate(
            [w[0, :, part] for w in weights] + [w[1, :, part] for w in weights], axis=0
        )
        wide = jnp.concatenate([signals[0, part, :], signals[1, part, :]], axis=1)
        product = jnp.dot(stack, wide, preferred_element_type=jnp.float32)
        if start:
            total[...] += product
        else:
            total[...] = product
    rows, samples = total.shape[0] // 2, signals.shape[2]
    out[0] = (total[:rows, :samples] - total[rows:, samples:]).astype(jnp.bfloat16)
    out[1] = (total[:rows, samples:] + total[rows:, :samples]).astype(jnp.bfloat16)


def form_beams(weights, signals):
    pieces = len(weights)
    rows, elements = weights[0].shape[1:]
    samples = signals.shape[2]
    all_rows = pieces * rows
    whole = pl.BlockSpec(memory_space=pltpu.VMEM)
    return pl.pallas_call(
        functools.partial(beams_kernel, pieces),
        in_specs=[whole] * (pieces + 1),
        out_specs=whole,
        out_shape=jax.ShapeDtypeStruct((2, all_rows, samples), jnp.bfloat16),
        scratch_shapes=[pltpu.VMEM((2 * all_rows, 2 * samples), jnp.float32)],
        compiler_params=pltpu.CompilerParams(vmem_limit_bytes=24 * MEBI),
        cost_estimate=pl.CostEstimate(
            flops=8 * all_rows * elements * samples,
            bytes_accessed=4 * elements * (all_rows + samples),
            transcendentals=0,
        ),
        name="form_beams",
    )(*weights, signals)


def order_kernel(parts, *refs):
    select, beams, out = refs[0], refs[1 : 1 + parts], refs[-1]
    real = jnp.concatenate([b[0] for b in beams], axis=0)
    imag = jnp.concatenate([b[1] for b in beams], axis=0)
    both = jnp.concatenate([real, imag], axis=1)
    samples = real.shape[1]
    for d in range(select.shape[0]):
        picked = jnp.dot(select[d], both, preferred_element_type=jnp.float32)
        out[d, 0] = picked[:, :samples].astype(jnp.bfloat16)
        out[d, 1] = picked[:, samples:].astype(jnp.bfloat16)


def order_beams(select, beams):
    tiles, rows, count = select.shape
    samples = beams[0].shape[2]
    whole = pl.BlockSpec(memory_space=pltpu.VMEM)
    return pl.pallas_call(
        functools.partial(order_kernel, len(beams)),
        in_specs=[whole] * (1 + len(beams)),
        out_specs=whole,
        out_shape=jax.ShapeDtypeStruct((tiles, 2, rows, samples), jnp.bfloat16),
        compiler_params=pltpu.CompilerParams(vmem_limit_bytes=24 * MEBI),
        cost_estimate=pl.CostEstimate(
            flops=4 * tiles * rows * count * samples,
            bytes_accessed=2 * tiles * rows * (count + 2 * samples),
            transcendentals=0,
        ),
        name="order_beams",
    )(select, *beams)


def bit_gaps(real, imag, index, scratch):
    shift = 8.0 * LEVEL * LEVEL
    for axis, field in ((0, real), (1, imag)):
        step = field * (2.0 * LEVEL)
        triple = field * (6.0 * LEVEL)
        scratch[axis * 4] = shift + triple
        scratch[axis * 4 + 1] = step
        scratch[axis * 4 + 2] = -step
        scratch[axis * 4 + 3] = shift - triple
    far = [scratch[index[label]] + scratch[index[16 + label]] for label in range(16)]
    least = jnp.minimum
    low = [
        least(least(far[b], far[b + 4]), least(far[b + 8], far[b + 12])) for b in range(4)
    ]
    high = [
        least(least(far[4 * b], far[4 * b + 1]), least(far[4 * b + 2], far[4 * b + 3]))
        for b in range(4)
    ]
    gaps = []
    for part in (low, high):
        gaps.append(least(part[1], part[3]) - least(part[0], part[2]))
        gaps.append(least(part[2], part[3]) - least(part[0], part[1]))
    return gaps


def expand(signs, coefs, base):
    terms = [coefs[base + t] + signs[3] * coefs[base + t + 8] for t in range(8)]
    terms = [terms[t] + signs[2] * terms[t + 4] for t in range(4)]
    terms = [terms[t] + signs[1] * terms[t + 2] for t in range(2)]
    return terms[0] + signs[0] * terms[1]


def soft_kernel(shape, index, field, first, second, scale, coefs, out, s_one, s_two, rest, scratch):
    blocks, rows, inner, tile = shape
    margin = (rows - inner) // 2
    dot = functools.partial(jnp.dot, preferred_element_type=jnp.float32)
    chunk = 16

    def tiles(value):
        return value.reshape(chunk // 8, 8, LANES)

    def soften(real, imag, start, slot):
        gaps = bit_gaps(real, imag, index, scratch.at[slot])
        half = tiles(scale[pl.ds(start, chunk), :])
        signs = [jnp.tanh(gap * half) for gap in gaps]
        return [
            expand(signs, coefs, base).reshape(chunk, LANES).astype(jnp.bfloat16)
            for base in (0, 16)
        ]

    width = first.shape[1] // 2

    @pl.when(pl.program_id(0) == 0)
    def _():
        s_one[...] = jnp.zeros_like(s_one)
        s_two[...] = jnp.zeros_like(s_two)

    count = 0
    for block in range(blocks):
        lanes = pl.ds(block * LANES, LANES)
        for start in range(0, rows, chunk):
            real = tiles(field[block, 0, start : start + chunk, :].astype(jnp.float32))
            imag = tiles(field[block, 1, start : start + chunk, :].astype(jnp.float32))
            a, b = soften(real, imag, start, count % 2)
            s_one[start : start + chunk, lanes] = a
            s_one[width + start : width + start + chunk, lanes] = b
            count += 1
    rest[...] = dot(first[...], s_one[...])
    for block in range(blocks):
        lanes = pl.ds(block * LANES, LANES)
        for start in range(0, inner, chunk):
            away = start + margin
            real = field[block, 0, away : away + chunk, :].astype(jnp.float32) - rest[
                start : start + chunk, lanes
            ]
            imag = field[block, 1, away : away + chunk, :].astype(jnp.float32) - rest[
                inner + start : inner + start + chunk, lanes
            ]
            a, b = soften(tiles(real), tiles(imag), away, count % 2)
            s_two[start : start + chunk, lanes] = a
            s_two[width + start : width + start + chunk, lanes] = b
            count += 1
    rest[0 : 2 * tile, :] = dot(second[...], s_two[...])
    for block in range(blocks):
        lanes = pl.ds(block * LANES, LANES)
        for start in range(0, tile, chunk):
            away = start + 2 * margin
            real = field[block, 0, away : away + chunk, :].astype(jnp.float32) - rest[
                start : start + chunk, lanes
            ]
            imag = field[block, 1, away : away + chunk, :].astype(jnp.float32) - rest[
                tile + start : tile + start + chunk, lanes
            ]
            gaps = bit_gaps(tiles(real), tiles(imag), index, scratch.at[count % 2])
            whole = 2.0 * tiles(scale[away : away + chunk, :])
            for bit in range(4):
                out[bit, start : start + chunk, lanes] = (
                    (gaps[bit] * whole).reshape(chunk, LANES).astype(jnp.bfloat16)
                )
            count += 1


def cancel(index, field, first, second, scale, coefs):
    sources, _, rows, samples = field.shape
    inner, tile = first.shape[0] // 2, second.shape[0] // 2
    blocks = 2
    wide = blocks * samples
    elements = sources * samples
    return pl.pallas_call(
        functools.partial(soft_kernel, (blocks, rows, inner, tile)),
        grid=(sources // blocks,),
        in_specs=[
            pl.BlockSpec(memory_space=pltpu.SMEM),
            pl.BlockSpec((blocks, 2, rows, samples), lambda s: (s, 0, 0, 0)),
            pl.BlockSpec(first.shape, lambda s: (0, 0)),
            pl.BlockSpec(second.shape, lambda s: (0, 0)),
            pl.BlockSpec(scale.shape, lambda s: (0, 0)),
            pl.BlockSpec(coefs.shape, lambda s: (0, 0, 0)),
        ],
        out_specs=pl.BlockSpec((4, tile, wide), lambda s: (0, 0, s)),
        out_shape=jax.ShapeDtypeStruct((4, tile, elements), jnp.bfloat16),
        scratch_shapes=[
            pltpu.VMEM((first.shape[1], wide), jnp.bfloat16),
            pltpu.VMEM((second.shape[1], wide), jnp.bfloat16),
            pltpu.VMEM((2 * inner, wide), jnp.float32),
            pltpu.VMEM((2, 8, 2, 8, LANES), jnp.float32),
        ],
        compiler_params=pltpu.CompilerParams(vmem_limit_bytes=24 * MEBI),
        cost_estimate=pl.CostEstimate(
            flops=130 * (rows + inner + tile) * elements,
            bytes_accessed=4 * rows * elements + 8 * tile * elements,
            transcendentals=4 * (rows + inner) * elements,
        ),
        name="cancel",
    )(index, field, first, second, scale, coefs)


class Places:
    def __init__(self, mesh):
        self.tm, self.beam = mesh.shape["tm"], mesh.shape["beam"]
        self.square = self.tm == 4 and self.beam == 8

    def flat(self, y, x, z, core):
        return (y * 2 + x) * self.beam + z * 2 + core

    def swap(self, value, y=0, x=0, z=0, core=0):
        mask = self.flat(y, x, z, core)
        pairs = [(i, i ^ mask) for i in range(self.tm * self.beam)]
        return lax.ppermute(value, ("tm", "beam"), pairs)


def after(value, *others):
    return lax.optimization_barrier((value, *others))[0]


MASKS = [(y, x, z, core) for z in (0, 2) for y in range(2) for x in range(2) for core in range(2)]


def rows_held(places, rows):
    if not places.square:
        return jnp.arange(places.tm * places.beam * rows, dtype=jnp.int32)
    masks = [places.flat(y, x, z ^ near, core) for near in (0, 1) for y, x, z, core in MASKS]
    me = lax.axis_index("tm") * places.beam + lax.axis_index("beam")
    source = me ^ np.array(masks, np.int32)
    held = source[:, None] * rows + jnp.arange(rows, dtype=jnp.int32)[None, :]
    return held.reshape(-1)


def all_beams(places, element_signals, beam_weights, ready):
    if not places.square:
        gathered = lax.all_gather(beam_weights, ("tm", "beam"), axis=1, tiled=True)
        return [form_beams([gathered], element_signals)]
    swap, w = places.swap, beam_weights
    w_z, w_x, w_y = swap(w, z=2), swap(w, x=1), swap(w, y=1)
    far = swap(after(element_signals, *ready), z=1)
    w_xy = swap(after(w_x, w_y), y=1)
    w_xz, w_yz = swap(after(w_z, w_y), x=1), swap(after(w_z, w_y), y=1)
    w_c, w_xc = swap(after(w, w_z), core=1), swap(after(w_x, w_z), core=1)
    w_yc, w_zc = swap(after(w_y, w_xy), core=1), swap(after(w_z, w_xy), core=1)
    w_xyc = swap(after(w_xy, w_zc), core=1)
    w_xyz = swap(after(w_yz, w_xz), x=1)
    w_xzc = swap(after(w_xz, w_xyc), core=1)
    w_yzc = swap(after(w_yz, w_xyc), core=1)
    w_xyzc = swap(w_xyz, core=1)
    pieces = [w, w_c, w_x, w_xc, w_y, w_yc, w_xy, w_xyc]
    pieces += [w_z, w_zc, w_xz, w_xzc, w_yz, w_yzc, w_xyz, w_xyzc]
    mine = form_beams(pieces, element_signals)
    other = form_beams(pieces, after(far, mine))
    return [mine, swap(other, z=1)]


def tables_kernel(shape, labels, taken, own, index, coefs, first, second, scale):
    slots, rows, inner, tile = shape
    margin = (rows - inner) // 2
    term = lax.broadcasted_iota(jnp.int32, (16, LANES), 0)
    sums = [jnp.zeros((16, LANES), jnp.float32) for _ in range(2)]
    for point in range(16):
        label = labels[point]
        index[label] = point // 4
        index[16 + label] = 4 + point % 4
        odd = term & label
        odd = odd ^ (odd >> 2)
        odd = (odd ^ (odd >> 1)) & 1
        sign = (1 - 2 * odd).astype(jnp.float32)
        for axis, step in ((0, point // 4), (1, point % 4)):
            sums[axis] += sign * ((2 * step - 3) * LEVEL / 16.0)
    for axis in range(2):
        for t in range(16):
            coefs[axis * 16 + t] = jnp.broadcast_to(sums[axis][t : t + 1, :], (8, LANES))
    scale[...] = jnp.broadcast_to(0.5 / taken[:, 3 * slots : 3 * slots + 1], scale.shape)

    def matrix(out, skip, height, which):
        beams = jnp.broadcast_to(own[which : which + 1, :], (height, own.shape[1]))
        real = jnp.zeros(beams.shape, jnp.float32)
        imag = jnp.zeros(beams.shape, jnp.float32)
        for k in range(slots):
            near, r, i = (
                taken[skip : skip + height, g * slots + k : g * slots + k + 1] for g in range(3)
            )
            hit = near == beams
            real += jnp.where(hit, r, 0.0)
            imag += jnp.where(hit, i, 0.0)
        width = own.shape[1]
        out[:height, :width] = real.astype(jnp.bfloat16)
        out[:height, width:] = (-imag).astype(jnp.bfloat16)
        out[height:, :width] = imag.astype(jnp.bfloat16)
        out[height:, width:] = real.astype(jnp.bfloat16)

    matrix(first, margin, inner, 0)
    matrix(second, 2 * margin, tile, 1)


def tables(bit_labels, taken, own, slots, tile):
    rows, width = taken.shape[0], own.shape[1]
    inner = rows - 2 * COLS
    vmem, smem = (pl.BlockSpec(memory_space=m) for m in (pltpu.VMEM, pltpu.SMEM))
    return pl.pallas_call(
        functools.partial(tables_kernel, (slots, rows, inner, tile)),
        in_specs=[smem, vmem, vmem],
        out_specs=[smem, vmem, vmem, vmem, vmem],
        out_shape=[
            jax.ShapeDtypeStruct((32,), jnp.int32),
            jax.ShapeDtypeStruct((32, 8, LANES), jnp.float32),
            jax.ShapeDtypeStruct((2 * inner, 2 * width), jnp.bfloat16),
            jax.ShapeDtypeStruct((2 * tile, 2 * width), jnp.bfloat16),
            jax.ShapeDtypeStruct((rows, LANES), jnp.float32),
        ],
        compiler_params=pltpu.CompilerParams(vmem_limit_bytes=16 * MEBI),
        cost_estimate=pl.CostEstimate(
            flops=60 * rows * width, bytes_accessed=16 * rows * width, transcendentals=0
        ),
        name="tables",
    )(bit_labels, taken, own)


def on_device(places, element_signals, beam_weights, beam_order, neighbours, leakage, noise_var, bit_labels):
    count = beam_order.shape[0]
    tile = count // places.beam
    rows = tile + 2 * HALO
    slots = neighbours.shape[1]
    padded = jnp.pad(beam_order, (HALO, HALO), constant_values=-1)
    windows = jnp.stack([padded[d * tile : d * tile + rows] for d in range(places.beam)])
    own = lax.dynamic_slice_in_dim(padded, lax.axis_index("beam") * tile, rows)
    width = -(-rows // LANES) * LANES
    sides = jnp.stack(
        [
            jnp.pad(own, (0, width - rows), constant_values=-1),
            jnp.pad(own[COLS:-COLS], (0, width - rows + 2 * COLS), constant_values=-1),
        ]
    ).astype(jnp.float32)
    table = jnp.concatenate(
        [
            neighbours.astype(jnp.float32),
            leakage[0].astype(jnp.float32),
            leakage[1].astype(jnp.float32),
            noise_var[:, None],
        ],
        axis=1,
    )
    taken = jnp.take(table, own, axis=0, mode="clip")
    index, coefs, first, second, scale = tables(bit_labels, taken, sides, slots, tile)
    held = rows_held(places, beam_weights.shape[1])
    select = (windows[:, :, None] == held[None, None, :]).astype(jnp.bfloat16)
    beams = all_beams(places, element_signals, beam_weights, (select, first, second))
    ordered = order_beams(select, beams)
    field = lax.all_to_all(ordered, "beam", split_axis=0, concat_axis=0, tiled=True)
    return cancel(index, field, first, second, scale, coefs)


def solution(mesh):
    in_specs = (
        P(None, None, ("tm", "beam")),
        P(None, ("tm", "beam"), None),
        P(),
        P(),
        P(),
        P(),
        P(),
    )
    return jax.shard_map(
        functools.partial(on_device, Places(mesh)),
        mesh=mesh,
        in_specs=in_specs,
        out_specs=P(None, "beam", "tm"),
        check_vma=False,
    )
```

```python
import functools
import itertools
import math

import jax
import jax.numpy as jnp
import numpy as np
from jax import lax
from jax.experimental import pallas as pl
from jax.experimental.pallas import tpu as pltpu
from jax.sharding import PartitionSpec as P

COLS = 16
HALO = 2 * COLS
LEVEL = 0.31622776601683794
LANES = 128
MEBI = 1 << 20


def beams_kernel(pieces, *refs):
    weights, signals, out, total = refs[:pieces], *refs[pieces:]
    elements = weights[0].shape[2]
    depth = math.gcd(elements, 512)
    for start in range(0, elements, depth):
        part = slice(start, start + depth)
        stack = jnp.concatenate(
            [w[0, :, part] for w in weights] + [w[1, :, part] for w in weights], axis=0
        )
        wide = jnp.concatenate([signals[0, part, :], signals[1, part, :]], axis=1)
        product = jnp.dot(stack, wide, preferred_element_type=jnp.float32)
        if start:
            total[...] += product
        else:
            total[...] = product
    rows, samples = total.shape[0] // 2, signals.shape[2]
    out[0] = (total[:rows, :samples] - total[rows:, samples:]).astype(jnp.bfloat16)
    out[1] = (total[:rows, samples:] + total[rows:, :samples]).astype(jnp.bfloat16)


def form_beams(weights, signals):
    pieces = len(weights)
    rows, elements = weights[0].shape[1:]
    samples = signals.shape[2]
    all_rows = pieces * rows
    whole = pl.BlockSpec(memory_space=pltpu.VMEM)
    return pl.pallas_call(
        functools.partial(beams_kernel, pieces),
        in_specs=[whole] * (pieces + 1),
        out_specs=whole,
        out_shape=jax.ShapeDtypeStruct((2, all_rows, samples), jnp.bfloat16),
        scratch_shapes=[pltpu.VMEM((2 * all_rows, 2 * samples), jnp.float32)],
        compiler_params=pltpu.CompilerParams(vmem_limit_bytes=12 * MEBI),
        cost_estimate=pl.CostEstimate(
            flops=8 * all_rows * elements * samples,
            bytes_accessed=4 * elements * (all_rows + samples),
            transcendentals=0,
        ),
        name="form_beams",
    )(*weights, signals)


def order_kernel(parts, *refs):
    select, beams, outs = refs[0], refs[1 : 1 + parts], refs[1 + parts :]
    real = jnp.concatenate([b[0] for b in beams], axis=0)
    imag = jnp.concatenate([b[1] for b in beams], axis=0)
    both = jnp.concatenate([real, imag], axis=1)
    samples = real.shape[1]
    for d, out in enumerate(outs):
        picked = jnp.dot(select[d], both, preferred_element_type=jnp.float32)
        out[0] = picked[:, :samples].astype(jnp.bfloat16)
        out[1] = picked[:, samples:].astype(jnp.bfloat16)


def order_beams(select, beams):
    tiles, rows, count = select.shape
    samples = beams[0].shape[2]
    whole = pl.BlockSpec(memory_space=pltpu.VMEM)
    return pl.pallas_call(
        functools.partial(order_kernel, len(beams)),
        in_specs=[whole] * (1 + len(beams)),
        out_specs=[whole] * tiles,
        out_shape=[jax.ShapeDtypeStruct((2, rows, samples), jnp.bfloat16)] * tiles,
        compiler_params=pltpu.CompilerParams(vmem_limit_bytes=12 * MEBI),
        cost_estimate=pl.CostEstimate(
            flops=4 * tiles * rows * count * samples,
            bytes_accessed=2 * tiles * rows * (count + 2 * samples),
            transcendentals=0,
        ),
        name="order_beams",
    )(select, *beams)


def bit_gaps(real, imag, step, shift, index, scratch):
    for axis, field in ((0, real), (1, imag)):
        near = field * step
        triple = near * 3.0
        scratch[axis * 4] = shift + triple
        scratch[axis * 4 + 1] = near
        scratch[axis * 4 + 2] = -near
        scratch[axis * 4 + 3] = shift - triple
    far = [scratch[index[label]] + scratch[index[16 + label]] for label in range(16)]
    least = jnp.minimum
    low = [
        least(least(far[b], far[b + 4]), least(far[b + 8], far[b + 12])) for b in range(4)
    ]
    high = [
        least(least(far[4 * b], far[4 * b + 1]), least(far[4 * b + 2], far[4 * b + 3]))
        for b in range(4)
    ]
    gaps = []
    for part in (low, high):
        gaps.append(least(part[1], part[3]) - least(part[0], part[2]))
        gaps.append(least(part[2], part[3]) - least(part[0], part[1]))
    return gaps


def expand(signs, coefs, base):
    terms = [coefs[base + t] + signs[3] * coefs[base + t + 8] for t in range(8)]
    terms = [terms[t] + signs[2] * terms[t + 4] for t in range(4)]
    terms = [terms[t] + signs[1] * terms[t + 2] for t in range(2)]
    return terms[0] + signs[0] * terms[1]


def cancel_kernel(shape, place, index, *refs):
    blocks, rows, inner, tile = shape
    fields, refs = refs[:blocks], refs[blocks:]
    first, second, scale, coefs = refs[:4]
    out, s_one, s_two, r_one, r_two = refs[-9:-4]
    spare = itertools.cycle(refs[-4:])
    margin = (rows - inner) // 2
    width = first.shape[1] // 2
    chunk = 16
    dot = functools.partial(jnp.dot, preferred_element_type=jnp.float32)

    def tiles(value):
        return value.reshape(chunk // 8, 8, LANES)

    def gaps_at(block, start, rest=None, row=0, height=0):
        parts = []
        for part in range(2):
            value = fields[block][part, pl.ds(start, chunk), :].astype(jnp.float32)
            if rest is not None:
                value = value - rest[block, pl.ds(part * height + row, chunk), :]
            parts.append(tiles(value))
        step, shift = (tiles(scale[i, pl.ds(start, chunk), :]) for i in range(2))
        return bit_gaps(*parts, step, shift, index, next(spare))

    def soften(block, out_ref, row, gaps):
        signs = [jnp.tanh(gap) for gap in gaps]
        for part in range(2):
            value = expand(signs, coefs, 16 * part).reshape(chunk, LANES)
            out_ref[block, pl.ds(part * width + row, chunk), :] = value.astype(jnp.bfloat16)

    def over(height, body):
        def step(i, carry):
            for part in range(2):
                row = pl.multiple_of((2 * i + part) * chunk, chunk)
                for block in range(blocks):
                    body(block, row)
            return carry

        lax.fori_loop(0, height // (2 * chunk), step, 0)

    for ref, used_rows in ((s_one, rows), (s_two, inner)):
        if used_rows < width:
            blank = jnp.zeros((width - used_rows, LANES), jnp.bfloat16)
            for block in range(blocks):
                ref[block, used_rows:width, :] = blank
                ref[block, width + used_rows :, :] = blank

    def first_round(block, row):
        soften(block, s_one, row, gaps_at(block, row))

    def second_round(block, row):
        soften(block, s_two, row, gaps_at(block, row + margin, r_one, row, inner))

    def metrics(block, row):
        core = place[1] if block == 0 else 1 - place[1]
        lanes = pl.ds(pl.multiple_of(core * LANES, LANES), LANES)
        gaps = gaps_at(block, row + 2 * margin, r_two, row, tile)
        for bit in range(4):
            value = (gaps[bit] * 2.0).reshape(chunk, LANES)
            out[bit, pl.ds(row, chunk), lanes] = value.astype(jnp.bfloat16)

    def product(matrix, ref, into):
        both = jnp.concatenate([ref[block] for block in range(blocks)], axis=1)
        result = dot(matrix[...], both)
        for block in range(blocks):
            into[block] = result[:, block * LANES : (block + 1) * LANES]

    over(rows, first_round)
    product(first, s_one, r_one)
    over(inner, second_round)
    product(second, s_two, r_two)
    over(tile, metrics)


def cancel(place, index, fields, first, second, scale, coefs, elements, before):
    _, rows, samples = fields[0].shape
    inner, tile = first.shape[0] // 2, second.shape[0] // 2
    blocks = len(fields)
    vmem, smem = (pl.BlockSpec(memory_space=m) for m in (pltpu.VMEM, pltpu.SMEM))
    given = [] if before is None else [before]
    wide = blocks * samples
    return pl.pallas_call(
        functools.partial(cancel_kernel, (blocks, rows, inner, tile)),
        grid_spec=pltpu.PrefetchScalarGridSpec(
            num_scalar_prefetch=1,
            grid=(1,),
            in_specs=[smem] + [vmem] * (blocks + 4) + [pl.BlockSpec(memory_space=pl.ANY)] * len(given),
            out_specs=pl.BlockSpec((4, tile, wide), lambda s, place: (0, 0, place[0])),
            scratch_shapes=[
                pltpu.VMEM((blocks, first.shape[1], samples), jnp.bfloat16),
                pltpu.VMEM((blocks, second.shape[1], samples), jnp.bfloat16),
                pltpu.VMEM((blocks, 2 * inner, samples), jnp.float32),
                pltpu.VMEM((blocks, 2 * tile, samples), jnp.float32),
            ]
            + [pltpu.VMEM((8, 2, 8, LANES), jnp.float32)] * 4,
        ),
        out_shape=jax.ShapeDtypeStruct((4, tile, elements), jnp.bfloat16),
        input_output_aliases={6 + blocks: 0} if given else {},
        compiler_params=pltpu.CompilerParams(vmem_limit_bytes=12 * MEBI),
        cost_estimate=pl.CostEstimate(
            flops=130 * (rows + inner + tile) * wide + 8 * inner * rows * wide,
            bytes_accessed=4 * rows * wide + 8 * tile * wide,
            transcendentals=4 * (rows + inner) * wide,
        ),
        name="cancel",
    )(place, index, *fields, first, second, scale, coefs, *given)


class Places:
    def __init__(self, mesh):
        self.tm, self.beam = mesh.shape["tm"], mesh.shape["beam"]
        self.square = self.tm == 4 and self.beam == 8

    def flat(self, y, x, z, core):
        return (y * 2 + x) * self.beam + z * 2 + core

    def swap(self, value, y=0, x=0, z=0, core=0):
        mask = self.flat(y, x, z, core)
        pairs = [(i, i ^ mask) for i in range(self.tm * self.beam)]
        return lax.ppermute(value, ("tm", "beam"), pairs)

    def shift(self, value, z, core):
        pairs = [(i, ((i + 2 * z) % self.beam) ^ core) for i in range(self.beam)]
        return lax.ppermute(value, "beam", pairs)


def after(value, *others):
    return lax.optimization_barrier((value, *others))[0]


MASKS = [(y, x, z, core) for z in (0, 2) for y in range(2) for x in range(2) for core in range(2)]


def rows_held(places, rows):
    if not places.square:
        return jnp.arange(places.tm * places.beam * rows, dtype=jnp.int32)
    masks = [places.flat(y, x, z ^ near, core) for near in (0, 1) for y, x, z, core in MASKS]
    me = lax.axis_index("tm") * places.beam + lax.axis_index("beam")
    source = me ^ np.array(masks, np.int32)
    held = source[:, None] * rows + jnp.arange(rows, dtype=jnp.int32)[None, :]
    return held.reshape(-1)


def all_beams(places, element_signals, beam_weights, ready):
    if not places.square:
        gathered = lax.all_gather(beam_weights, ("tm", "beam"), axis=1, tiled=True)
        return form_beams([gathered], element_signals), None
    swap, w = places.swap, beam_weights
    w_z, w_x, w_y = swap(w, z=2), swap(w, x=1), swap(w, y=1)
    far = swap(after(element_signals, *ready), z=1)
    w_xy = swap(after(w_x, w_y), y=1)
    w_xz, w_yz = swap(after(w_z, w_y), x=1), swap(after(w_z, w_y), y=1)
    w_c, w_xc = swap(after(w, w_z), core=1), swap(after(w_x, w_z), core=1)
    w_yc, w_zc = swap(after(w_y, w_xy), core=1), swap(after(w_z, w_xy), core=1)
    w_xyc = swap(after(w_xy, w_zc), core=1)
    w_xyz = swap(after(w_yz, w_xz), x=1)
    w_xzc = swap(after(w_xz, w_xyc), core=1)
    w_yzc = swap(after(w_yz, w_xyc), core=1)
    w_xyzc = swap(w_xyz, core=1)
    pieces = [w, w_c, w_x, w_xc, w_y, w_yc, w_xy, w_xyc]
    pieces += [w_z, w_zc, w_xz, w_xzc, w_yz, w_yzc, w_xyz, w_xyzc]
    mine = form_beams(pieces, element_signals)
    other = form_beams(pieces, after(far, mine))
    return mine, other


def tables_kernel(shape, labels, taken, own, index, coefs, first, second, scale):
    slots, rows, inner, tile = shape
    margin = (rows - inner) // 2
    term = lax.broadcasted_iota(jnp.int32, (16, LANES), 0)
    sums = [jnp.zeros((16, LANES), jnp.float32) for _ in range(2)]
    for point in range(16):
        label = labels[point]
        index[label] = point // 4
        index[16 + label] = 4 + point % 4
        odd = term & label
        odd = odd ^ (odd >> 2)
        odd = (odd ^ (odd >> 1)) & 1
        sign = (1 - 2 * odd).astype(jnp.float32)
        for axis, step in ((0, point // 4), (1, point % 4)):
            sums[axis] += sign * ((2 * step - 3) * LEVEL / 16.0)
    for axis in range(2):
        for t in range(16):
            coefs[axis * 16 + t] = jnp.broadcast_to(sums[axis][t : t + 1, :], (8, LANES))
    half = jnp.broadcast_to(0.5 / taken[:, 3 * slots : 3 * slots + 1], scale.shape[1:])
    scale[0] = half * (2.0 * LEVEL)
    scale[1] = half * (8.0 * LEVEL * LEVEL)

    def matrix(out, skip, height, which):
        beams = jnp.broadcast_to(own[which : which + 1, :], (height, own.shape[1]))
        real = jnp.zeros(beams.shape, jnp.float32)
        imag = jnp.zeros(beams.shape, jnp.float32)
        for k in range(slots):
            near, r, i = (
                taken[skip : skip + height, g * slots + k : g * slots + k + 1] for g in range(3)
            )
            hit = near == beams
            real += jnp.where(hit, r, 0.0)
            imag += jnp.where(hit, i, 0.0)
        width = own.shape[1]
        out[:height, :width] = real.astype(jnp.bfloat16)
        out[:height, width:] = (-imag).astype(jnp.bfloat16)
        out[height:, :width] = imag.astype(jnp.bfloat16)
        out[height:, width:] = real.astype(jnp.bfloat16)

    matrix(first, margin, inner, 0)
    matrix(second, 2 * margin, tile, 1)


def tables(bit_labels, taken, own, slots, tile):
    rows, width = taken.shape[0], own.shape[1]
    inner = rows - 2 * COLS
    vmem, smem = (pl.BlockSpec(memory_space=m) for m in (pltpu.VMEM, pltpu.SMEM))
    return pl.pallas_call(
        functools.partial(tables_kernel, (slots, rows, inner, tile)),
        in_specs=[smem, vmem, vmem],
        out_specs=[smem, vmem, vmem, vmem, vmem],
        out_shape=[
            jax.ShapeDtypeStruct((32,), jnp.int32),
            jax.ShapeDtypeStruct((32, 8, LANES), jnp.float32),
            jax.ShapeDtypeStruct((2 * inner, 2 * width), jnp.bfloat16),
            jax.ShapeDtypeStruct((2 * tile, 2 * width), jnp.bfloat16),
            jax.ShapeDtypeStruct((2, rows, LANES), jnp.float32),
        ],
        compiler_params=pltpu.CompilerParams(vmem_limit_bytes=12 * MEBI),
        cost_estimate=pl.CostEstimate(
            flops=60 * rows * width, bytes_accessed=16 * rows * width, transcendentals=0
        ),
        name="tables",
    )(bit_labels, taken, own)


def on_device(places, element_signals, beam_weights, beam_order, neighbours, leakage, noise_var, bit_labels):
    count = beam_order.shape[0]
    tile = count // places.beam
    rows = tile + 2 * HALO
    slots = neighbours.shape[1]
    padded = jnp.pad(beam_order, (HALO, HALO), constant_values=-1)
    windows = jnp.stack([padded[d * tile : d * tile + rows] for d in range(places.beam)])
    own = lax.dynamic_slice_in_dim(padded, lax.axis_index("beam") * tile, rows)
    width = -(-rows // LANES) * LANES
    sides = jnp.stack(
        [
            jnp.pad(own, (0, width - rows), constant_values=-1),
            jnp.pad(own[COLS:-COLS], (0, width - rows + 2 * COLS), constant_values=-1),
        ]
    ).astype(jnp.float32)
    table = jnp.concatenate(
        [
            neighbours.astype(jnp.float32),
            leakage[0].astype(jnp.float32),
            leakage[1].astype(jnp.float32),
            noise_var[:, None],
        ],
        axis=1,
    )
    taken = jnp.take(table, own, axis=0, mode="clip")
    held = rows_held(places, beam_weights.shape[1])
    me = lax.axis_index("beam")
    if places.square:
        moves = [(0, 0), (0, 1), (1, 0), (1, 1), (3, 0), (3, 1), (2, 0), (2, 1)]
        z, core = (np.array(v, np.int32) for v in zip(*moves))
        windows = windows[((me + 2 * z) % places.beam) ^ core]
    select = (windows[:, :, None] == held[None, None, :]).astype(jnp.bfloat16)
    mine, other = all_beams(places, element_signals, beam_weights, (select, taken, sides))
    beams = [mine]
    if other is not None:
        beams.append(places.swap(other, z=1))
        taken = after(taken, other)
    index, coefs, first, second, scale = tables(bit_labels, taken, sides, slots, tile)
    select = after(select, first, second, scale, coefs)
    ordered = list(order_beams(select, beams))
    chips = places.beam // 2
    elements = element_signals.shape[2] * places.beam
    out = None
    if places.square:
        fields = ordered[:1] + [
            places.shift(value, *move) for value, move in zip(ordered[1:6], moves[1:6])
        ]
        spots = [((me // 2 - z) % chips, me % 2) for z, _ in moves[::2]]
    else:
        fields = list(
            lax.all_to_all(jnp.stack(ordered), "beam", split_axis=0, concat_axis=0, tiled=True)
        )
        spots = [(chip, 0) for chip in range(chips)]
    for i, spot in enumerate(spots):
        place = jnp.stack([jnp.asarray(v, jnp.int32) for v in spot])
        pair = fields[2 * i : 2 * i + 2]
        out = cancel(place, index, pair, first, second, scale, coefs, elements, out)
        if places.square and i == 0:
            fields += [places.shift(after(ordered[j], out), *moves[j]) for j in (6, 7)]
    return out


def solution(mesh):
    in_specs = (
        P(None, None, ("tm", "beam")),
        P(None, ("tm", "beam"), None),
        P(),
        P(),
        P(),
        P(),
        P(),
    )
    return jax.shard_map(
        functools.partial(on_device, Places(mesh)),
        mesh=mesh,
        in_specs=in_specs,
        out_specs=P(None, "beam", "tm"),
        check_vma=False,
    )
```

```python
import functools
import itertools
import math

import jax
import jax.numpy as jnp
import numpy as np
from jax import lax
from jax.experimental import pallas as pl
from jax.experimental.pallas import tpu as pltpu
from jax.sharding import PartitionSpec as P

COLS = 16
HALO = 2 * COLS
LEVEL = 0.31622776601683794
LANES = 128
MEBI = 1 << 20


def beams_kernel(pieces, *refs):
    weights, signals, out, total = refs[:pieces], *refs[pieces:]
    elements = weights[0].shape[2]
    depth = math.gcd(elements, 512)
    for start in range(0, elements, depth):
        part = slice(start, start + depth)
        stack = jnp.concatenate(
            [w[0, :, part] for w in weights] + [w[1, :, part] for w in weights], axis=0
        )
        wide = jnp.concatenate([signals[0, part, :], signals[1, part, :]], axis=1)
        product = jnp.dot(stack, wide, preferred_element_type=jnp.float32)
        if start:
            total[...] += product
        else:
            total[...] = product
    rows, samples = total.shape[0] // 2, signals.shape[2]
    out[0] = (total[:rows, :samples] - total[rows:, samples:]).astype(jnp.bfloat16)
    out[1] = (total[:rows, samples:] + total[rows:, :samples]).astype(jnp.bfloat16)


def form_beams(weights, signals):
    pieces = len(weights)
    rows, elements = weights[0].shape[1:]
    samples = signals.shape[2]
    all_rows = pieces * rows
    whole = pl.BlockSpec(memory_space=pltpu.VMEM)
    return pl.pallas_call(
        functools.partial(beams_kernel, pieces),
        in_specs=[whole] * (pieces + 1),
        out_specs=whole,
        out_shape=jax.ShapeDtypeStruct((2, all_rows, samples), jnp.bfloat16),
        scratch_shapes=[pltpu.VMEM((2 * all_rows, 2 * samples), jnp.float32)],
        compiler_params=pltpu.CompilerParams(vmem_limit_bytes=12 * MEBI),
        cost_estimate=pl.CostEstimate(
            flops=8 * all_rows * elements * samples,
            bytes_accessed=4 * elements * (all_rows + samples),
            transcendentals=0,
        ),
        name="form_beams",
    )(*weights, signals)


def order_kernel(parts, *refs):
    select, beams, outs = refs[0], refs[1 : 1 + parts], refs[1 + parts :]
    real = jnp.concatenate([b[0] for b in beams], axis=0)
    imag = jnp.concatenate([b[1] for b in beams], axis=0)
    both = jnp.concatenate([real, imag], axis=1)
    samples = real.shape[1]
    for d, out in enumerate(outs):
        picked = jnp.dot(select[d], both, preferred_element_type=jnp.float32)
        out[0] = picked[:, :samples].astype(jnp.bfloat16)
        out[1] = picked[:, samples:].astype(jnp.bfloat16)


def order_beams(select, beams):
    tiles, rows, count = select.shape
    samples = beams[0].shape[2]
    whole = pl.BlockSpec(memory_space=pltpu.VMEM)
    return pl.pallas_call(
        functools.partial(order_kernel, len(beams)),
        in_specs=[whole] * (1 + len(beams)),
        out_specs=[whole] * tiles,
        out_shape=[jax.ShapeDtypeStruct((2, rows, samples), jnp.bfloat16)] * tiles,
        compiler_params=pltpu.CompilerParams(vmem_limit_bytes=12 * MEBI),
        cost_estimate=pl.CostEstimate(
            flops=4 * tiles * rows * count * samples,
            bytes_accessed=2 * tiles * rows * (count + 2 * samples),
            transcendentals=0,
        ),
        name="order_beams",
    )(select, *beams)


def bit_gaps(real, imag, step, shift, index, scratch):
    for axis, field in ((0, real), (1, imag)):
        near = field * step
        triple = near * 3.0
        scratch[axis * 4] = shift + triple
        scratch[axis * 4 + 1] = near
        scratch[axis * 4 + 2] = -near
        scratch[axis * 4 + 3] = shift - triple
    far = [scratch[index[label]] + scratch[index[16 + label]] for label in range(16)]
    least = jnp.minimum
    low = [
        least(least(far[b], far[b + 4]), least(far[b + 8], far[b + 12])) for b in range(4)
    ]
    high = [
        least(least(far[4 * b], far[4 * b + 1]), least(far[4 * b + 2], far[4 * b + 3]))
        for b in range(4)
    ]
    gaps = []
    for part in (low, high):
        gaps.append(least(part[1], part[3]) - least(part[0], part[2]))
        gaps.append(least(part[2], part[3]) - least(part[0], part[1]))
    return gaps


def expand(signs, coefs, base):
    terms = [coefs[base + t] + signs[3] * coefs[base + t + 8] for t in range(8)]
    terms = [terms[t] + signs[2] * terms[t + 4] for t in range(4)]
    terms = [terms[t] + signs[1] * terms[t + 2] for t in range(2)]
    return terms[0] + signs[0] * terms[1]


def cancel_kernel(shape, turn, place, index, *refs):
    blocks, rows, inner, tile = shape
    fields, refs = refs[:blocks], refs[blocks:]
    first, second, scale, coefs = refs[:4]
    out, s_one, s_two, r_one, r_two, ready, sent = refs[-11:-4]
    spare = itertools.cycle(refs[-4:])
    margin = (rows - inner) // 2
    width = first.shape[1] // 2
    chunk = 16
    mine = place[place.shape[0] - 1]
    skip = pl.multiple_of(mine * tile, chunk)
    dot = functools.partial(jnp.dot, preferred_element_type=jnp.float32)

    def tiles(value):
        return value.reshape(chunk // 8, 8, LANES)

    def gaps_at(block, start, rest=None, row=0, height=0):
        parts = []
        for part in range(2):
            value = fields[block][part, pl.ds(skip + start, chunk), :].astype(jnp.float32)
            if rest is not None:
                value = value - rest[block, pl.ds(part * height + row, chunk), :]
            parts.append(tiles(value))
        step, shift = (tiles(scale[i, pl.ds(start, chunk), :]) for i in range(2))
        return bit_gaps(*parts, step, shift, index, next(spare))

    def soften(block, out_ref, row, gaps):
        signs = [jnp.tanh(gap) for gap in gaps]
        for part in range(2):
            value = expand(signs, coefs, 16 * part).reshape(chunk, LANES)
            out_ref[block, pl.ds(part * width + row, chunk), :] = value.astype(jnp.bfloat16)

    def over(height, body, wanted=tuple(range(blocks))):
        parts = math.gcd(height // chunk, 4 // len(wanted))

        def step(i, carry):
            for part in range(parts):
                row = pl.multiple_of((parts * i + part) * chunk, chunk)
                for block in wanted:
                    body(block, row)
            return carry

        lax.fori_loop(0, height // (parts * chunk), step, 0)

    for ref, used_rows in ((s_one, rows), (s_two, inner)):
        if used_rows < width:
            blank = jnp.zeros((width - used_rows, LANES), jnp.bfloat16)
            for block in range(blocks):
                ref[block, used_rows:width, :] = blank
                ref[block, width + used_rows :, :] = blank

    def first_round(block, row):
        soften(block, s_one, row, gaps_at(block, row))

    def second_round(block, row):
        soften(block, s_two, row, gaps_at(block, row + margin, r_one, row, inner))

    def metrics(block, row):
        gaps = gaps_at(block, row + 2 * margin, r_two, row, tile)
        for bit in range(4):
            value = (gaps[bit] * 2.0).reshape(chunk, LANES)
            ready[block, bit, pl.ds(row, chunk), :] = value.astype(jnp.bfloat16)

    def send(block):
        lane = pl.multiple_of(place[blocks * turn + block] * LANES, LANES)
        target = out.at[:, :, pl.ds(lane, LANES)]
        return pltpu.make_async_copy(ready.at[block], target, sent.at[block])

    def product(matrix, ref, into):
        both = jnp.concatenate([ref[block] for block in range(blocks)], axis=1)
        result = dot(matrix[...], both)
        for block in range(blocks):
            into[block] = result[:, block * LANES : (block + 1) * LANES]

    over(rows, first_round)
    product(first, s_one, r_one)
    over(inner, second_round)
    product(second, s_two, r_two)
    for block in range(blocks):
        over(tile, metrics, (block,))
        send(block).start()
    for block in range(blocks):
        send(block).wait()


def cancel(turn, place, index, fields, first, second, scale, coefs, elements, before):
    samples = fields[0].shape[2]
    rows, inner, tile = scale.shape[1], first.shape[0] // 2, second.shape[0] // 2
    blocks = len(fields)
    vmem, smem = (pl.BlockSpec(memory_space=m) for m in (pltpu.VMEM, pltpu.SMEM))
    anywhere = pl.BlockSpec(memory_space=pl.ANY)
    given = [] if before is None else [before]
    wide = blocks * samples
    return pl.pallas_call(
        functools.partial(cancel_kernel, (blocks, rows, inner, tile), turn),
        in_specs=[smem] * 2 + [vmem] * (blocks + 4) + [anywhere] * len(given),
        out_specs=anywhere,
        scratch_shapes=[
            pltpu.VMEM((blocks, first.shape[1], samples), jnp.bfloat16),
            pltpu.VMEM((blocks, second.shape[1], samples), jnp.bfloat16),
            pltpu.VMEM((blocks, 2 * inner, samples), jnp.float32),
            pltpu.VMEM((blocks, 2 * tile, samples), jnp.float32),
            pltpu.VMEM((blocks, 4, tile, samples), jnp.bfloat16),
            pltpu.SemaphoreType.DMA((blocks,)),
        ]
        + [pltpu.VMEM((8, 2, 8, LANES), jnp.float32)] * 4,
        out_shape=jax.ShapeDtypeStruct((4, tile, elements), jnp.bfloat16),
        input_output_aliases={6 + blocks: 0} if given else {},
        compiler_params=pltpu.CompilerParams(vmem_limit_bytes=12 * MEBI),
        cost_estimate=pl.CostEstimate(
            flops=130 * (rows + inner + tile) * wide + 8 * inner * rows * wide,
            bytes_accessed=4 * rows * wide + 8 * tile * wide,
            transcendentals=4 * (rows + inner) * wide,
        ),
        name="cancel",
    )(place, index, *fields, first, second, scale, coefs, *given)


class Places:
    def __init__(self, mesh):
        self.tm, self.beam = mesh.shape["tm"], mesh.shape["beam"]
        self.square = self.tm == 4 and self.beam == 8

    def flat(self, y, x, z, core):
        return (y * 2 + x) * self.beam + z * 2 + core

    def swap(self, value, y=0, x=0, z=0, core=0):
        mask = self.flat(y, x, z, core)
        pairs = [(i, i ^ mask) for i in range(self.tm * self.beam)]
        return lax.ppermute(value, ("tm", "beam"), pairs)

    def shift(self, value, z):
        pairs = [(i, (i + 2 * z) % self.beam) for i in range(self.beam)]
        return lax.ppermute(value, "beam", pairs)


def after(value, *others):
    return lax.optimization_barrier((value, *others))[0]


MASKS = [(y, x, z, core) for z in (0, 2) for y in range(2) for x in range(2) for core in range(2)]


def rows_held(places, rows):
    if not places.square:
        return jnp.arange(places.tm * places.beam * rows, dtype=jnp.int32)
    masks = [places.flat(y, x, z ^ near, core) for near in (0, 1) for y, x, z, core in MASKS]
    me = lax.axis_index("tm") * places.beam + lax.axis_index("beam")
    source = me ^ np.array(masks, np.int32)
    held = source[:, None] * rows + jnp.arange(rows, dtype=jnp.int32)[None, :]
    return held.reshape(-1)


def all_beams(places, element_signals, beam_weights, ready):
    if not places.square:
        gathered = lax.all_gather(beam_weights, ("tm", "beam"), axis=1, tiled=True)
        return form_beams([gathered], element_signals), None
    swap, w = places.swap, beam_weights
    w_z, w_x, w_y = swap(w, z=2), swap(w, x=1), swap(w, y=1)
    far = swap(after(element_signals, *ready), z=1)
    w_xy = swap(after(w_x, w_y), y=1)
    w_xz, w_yz = swap(after(w_z, w_y), x=1), swap(after(w_z, w_y), y=1)
    w_c, w_xc = swap(after(w, w_z), core=1), swap(after(w_x, w_z), core=1)
    w_yc, w_zc = swap(after(w_y, w_xy), core=1), swap(after(w_z, w_xy), core=1)
    w_xyc = swap(after(w_xy, w_zc), core=1)
    w_xyz = swap(after(w_yz, w_xz), x=1)
    w_xzc = swap(after(w_xz, w_xyc), core=1)
    w_yzc = swap(after(w_yz, w_xyc), core=1)
    w_xyzc = swap(w_xyz, core=1)
    pieces = [w, w_c, w_x, w_xc, w_y, w_yc, w_xy, w_xyc]
    pieces += [w_z, w_zc, w_xz, w_xzc, w_yz, w_yzc, w_xyz, w_xyzc]
    mine = form_beams(pieces, element_signals)
    other = form_beams(pieces, after(far, mine))
    return mine, other


def tables_kernel(shape, labels, taken, own, index, coefs, first, second, scale):
    slots, rows, inner, tile = shape
    margin = (rows - inner) // 2
    term = lax.broadcasted_iota(jnp.int32, (16, LANES), 0)
    sums = [jnp.zeros((16, LANES), jnp.float32) for _ in range(2)]
    for point in range(16):
        label = labels[point]
        index[label] = point // 4
        index[16 + label] = 4 + point % 4
        odd = term & label
        odd = odd ^ (odd >> 2)
        odd = (odd ^ (odd >> 1)) & 1
        sign = (1 - 2 * odd).astype(jnp.float32)
        for axis, step in ((0, point // 4), (1, point % 4)):
            sums[axis] += sign * ((2 * step - 3) * LEVEL / 16.0)
    for axis in range(2):
        for t in range(16):
            coefs[axis * 16 + t] = jnp.broadcast_to(sums[axis][t : t + 1, :], (8, LANES))
    half = jnp.broadcast_to(0.5 / taken[:, 3 * slots : 3 * slots + 1], scale.shape[1:])
    scale[0] = half * (2.0 * LEVEL)
    scale[1] = half * (8.0 * LEVEL * LEVEL)

    def matrix(out, skip, height, which):
        beams = jnp.broadcast_to(own[which : which + 1, :], (height, own.shape[1]))
        real = jnp.zeros(beams.shape, jnp.float32)
        imag = jnp.zeros(beams.shape, jnp.float32)
        for k in range(slots):
            near, r, i = (
                taken[skip : skip + height, g * slots + k : g * slots + k + 1] for g in range(3)
            )
            hit = near == beams
            real += jnp.where(hit, r, 0.0)
            imag += jnp.where(hit, i, 0.0)
        width = own.shape[1]
        out[:height, :width] = real.astype(jnp.bfloat16)
        out[:height, width:] = (-imag).astype(jnp.bfloat16)
        out[height:, :width] = imag.astype(jnp.bfloat16)
        out[height:, width:] = real.astype(jnp.bfloat16)

    matrix(first, margin, inner, 0)
    matrix(second, 2 * margin, tile, 1)


def tables(bit_labels, taken, own, slots, tile):
    rows, width = taken.shape[0], own.shape[1]
    inner = rows - 2 * COLS
    vmem, smem = (pl.BlockSpec(memory_space=m) for m in (pltpu.VMEM, pltpu.SMEM))
    return pl.pallas_call(
        functools.partial(tables_kernel, (slots, rows, inner, tile)),
        in_specs=[smem, vmem, vmem],
        out_specs=[smem, vmem, vmem, vmem, vmem],
        out_shape=[
            jax.ShapeDtypeStruct((32,), jnp.int32),
            jax.ShapeDtypeStruct((32, 8, LANES), jnp.float32),
            jax.ShapeDtypeStruct((2 * inner, 2 * width), jnp.bfloat16),
            jax.ShapeDtypeStruct((2 * tile, 2 * width), jnp.bfloat16),
            jax.ShapeDtypeStruct((2, rows, LANES), jnp.float32),
        ],
        compiler_params=pltpu.CompilerParams(vmem_limit_bytes=12 * MEBI),
        cost_estimate=pl.CostEstimate(
            flops=60 * rows * width, bytes_accessed=16 * rows * width, transcendentals=0
        ),
        name="tables",
    )(bit_labels, taken, own)


def on_device(places, element_signals, beam_weights, beam_order, neighbours, leakage, noise_var, bit_labels):
    count = beam_order.shape[0]
    tile = count // places.beam
    rows = tile + 2 * HALO
    slots = neighbours.shape[1]
    width = -(-rows // LANES) * LANES
    padded = jnp.pad(beam_order, (HALO, width + COLS), constant_values=-1)
    group = 2 if places.square else 1
    reach = group * tile
    span = reach + 2 * HALO
    windows = [padded[i : i + count : 1] for i in range(0, span, reach)]
    windows = jnp.concatenate([v.reshape(-1, reach) for v in windows], axis=1)[:, :span]
    own = lax.dynamic_slice_in_dim(padded, lax.axis_index("beam") * tile, width + COLS)
    sides = jnp.stack([own[:width], own[COLS:]]).astype(jnp.float32)
    table = jnp.concatenate(
        [
            neighbours.astype(jnp.float32),
            leakage[0].astype(jnp.float32),
            leakage[1].astype(jnp.float32),
            noise_var[:, None],
        ],
        axis=1,
    )
    taken = jnp.take(table, own[:rows], axis=0, mode="clip")
    held = rows_held(places, beam_weights.shape[1])
    me = lax.axis_index("beam")
    chips = places.beam // 2
    moves = (0, 1, 3, 2)
    if places.square:
        windows = windows[(me // 2 + np.array(moves, np.int32)) % chips]
    select = (windows[:, :, None] == held[None, None, :]).astype(jnp.bfloat16)
    mine, other = all_beams(places, element_signals, beam_weights, (select, taken, sides))
    beams = [mine]
    if other is not None:
        beams.append(places.swap(other, z=1))
        taken = after(taken, other)
    index, coefs, first, second, scale = tables(bit_labels, taken, sides, slots, tile)
    select = after(select, first, second, scale, coefs)
    ordered = list(order_beams(select, beams))
    elements = element_signals.shape[2] * places.beam
    if places.square:
        here, *away = ordered
        one, three = places.shift(away[0], 1), places.shift(away[1], 3)
        pairs = [[here, places.swap(here, core=1)]]
        shifts = np.array([0, 0, 1, 3, 1, 3, 2, 2], np.int32)
        flips = np.array([0, 1, 0, 0, 1, 1, 0, 1], np.int32)
        place = (me - 2 * shifts) % places.beam ^ flips
        place = jnp.concatenate([place, (me % 2)[None]])
    else:
        fields = list(
            lax.all_to_all(jnp.stack(ordered), "beam", split_axis=0, concat_axis=0, tiled=True)
        )
        pairs = [fields[2 * i : 2 * i + 2] for i in range(chips)]
        place = jnp.arange(places.beam + 1, dtype=jnp.int32) % places.beam

    def run(turn, pair, before):
        return cancel(turn, place, index, pair, first, second, scale, coefs, elements, before)

    out = run(0, pairs[0], None)
    if places.square:
        two = places.shift(after(away[2], out), 2)
        one, three = after(one, out), after(three, out)
        far_one, far_three = places.swap(one, core=1), places.swap(three, core=1)
        out = run(1, [one, three], out)
        two = after(two, out)
        far_two = places.swap(two, core=1)
        out = run(2, [far_one, far_three], out)
        return run(3, [two, far_two], out)
    for i in range(1, chips):
        out = run(i, pairs[i], out)
    return out


def solution(mesh):
    in_specs = (
        P(None, None, ("tm", "beam")),
        P(None, ("tm", "beam"), None),
        P(),
        P(),
        P(),
        P(),
        P(),
    )
    return jax.shard_map(
        functools.partial(on_device, Places(mesh)),
        mesh=mesh,
        in_specs=in_specs,
        out_specs=P(None, "beam", "tm"),
        check_vma=False,
    )
```

```python
import functools
import itertools
import math

import jax
import jax.numpy as jnp
import numpy as np
from jax import lax
from jax.experimental import pallas as pl
from jax.experimental.pallas import tpu as pltpu
from jax.sharding import PartitionSpec as P

COLS = 16
HALO = 2 * COLS
LEVEL = 0.31622776601683794
LANES = 128
MEBI = 1 << 20


def beams_kernel(pieces, *refs):
    weights, signals, out, total = refs[:pieces], *refs[pieces:]
    elements = weights[0].shape[2]
    depth = math.gcd(elements, 512)
    for start in range(0, elements, depth):
        part = slice(start, start + depth)
        stack = jnp.concatenate(
            [w[0, :, part] for w in weights] + [w[1, :, part] for w in weights], axis=0
        )
        wide = jnp.concatenate([signals[0, part, :], signals[1, part, :]], axis=1)
        product = jnp.dot(stack, wide, preferred_element_type=jnp.float32)
        if start:
            total[...] += product
        else:
            total[...] = product
    rows, samples = total.shape[0] // 2, signals.shape[2]
    out[0] = (total[:rows, :samples] - total[rows:, samples:]).astype(jnp.bfloat16)
    out[1] = (total[:rows, samples:] + total[rows:, :samples]).astype(jnp.bfloat16)


def form_beams(weights, signals):
    pieces = len(weights)
    rows, elements = weights[0].shape[1:]
    samples = signals.shape[2]
    all_rows = pieces * rows
    whole = pl.BlockSpec(memory_space=pltpu.VMEM)
    return pl.pallas_call(
        functools.partial(beams_kernel, pieces),
        in_specs=[whole] * (pieces + 1),
        out_specs=whole,
        out_shape=jax.ShapeDtypeStruct((2, all_rows, samples), jnp.bfloat16),
        scratch_shapes=[pltpu.VMEM((2 * all_rows, 2 * samples), jnp.float32)],
        compiler_params=pltpu.CompilerParams(vmem_limit_bytes=12 * MEBI),
        cost_estimate=pl.CostEstimate(
            flops=8 * all_rows * elements * samples,
            bytes_accessed=4 * elements * (all_rows + samples),
            transcendentals=0,
        ),
        name="form_beams",
    )(*weights, signals)


def order_kernel(parts, *refs):
    select, beams, outs = refs[0], refs[1 : 1 + parts], refs[1 + parts :]
    real = jnp.concatenate([b[0] for b in beams], axis=0)
    imag = jnp.concatenate([b[1] for b in beams], axis=0)
    both = jnp.concatenate([real, imag], axis=1)
    samples = real.shape[1]
    for d, out in enumerate(outs):
        picked = jnp.dot(select[d], both, preferred_element_type=jnp.float32)
        out[0] = picked[:, :samples].astype(jnp.bfloat16)
        out[1] = picked[:, samples:].astype(jnp.bfloat16)


def order_beams(select, beams):
    tiles, rows, count = select.shape
    samples = beams[0].shape[2]
    whole = pl.BlockSpec(memory_space=pltpu.VMEM)
    return pl.pallas_call(
        functools.partial(order_kernel, len(beams)),
        in_specs=[whole] * (1 + len(beams)),
        out_specs=[whole] * tiles,
        out_shape=[jax.ShapeDtypeStruct((2, rows, samples), jnp.bfloat16)] * tiles,
        compiler_params=pltpu.CompilerParams(vmem_limit_bytes=12 * MEBI),
        cost_estimate=pl.CostEstimate(
            flops=4 * tiles * rows * count * samples,
            bytes_accessed=2 * tiles * rows * (count + 2 * samples),
            transcendentals=0,
        ),
        name="order_beams",
    )(select, *beams)


def bit_gaps(real, imag, step, shift, index, scratch):
    for axis, field in ((0, real), (1, imag)):
        near = field * step
        triple = near * 3.0
        scratch[axis * 4] = shift + triple
        scratch[axis * 4 + 1] = near
        scratch[axis * 4 + 2] = -near
        scratch[axis * 4 + 3] = shift - triple
    far = [scratch[index[label]] + scratch[index[16 + label]] for label in range(16)]
    least = jnp.minimum
    low = [
        least(least(far[b], far[b + 4]), least(far[b + 8], far[b + 12])) for b in range(4)
    ]
    high = [
        least(least(far[4 * b], far[4 * b + 1]), least(far[4 * b + 2], far[4 * b + 3]))
        for b in range(4)
    ]
    gaps = []
    for part in (low, high):
        gaps.append(least(part[1], part[3]) - least(part[0], part[2]))
        gaps.append(least(part[2], part[3]) - least(part[0], part[1]))
    return gaps


def expand(signs, coefs, base):
    terms = [coefs[base + t] + signs[3] * coefs[base + t + 8] for t in range(8)]
    terms = [terms[t] + signs[2] * terms[t + 4] for t in range(4)]
    terms = [terms[t] + signs[1] * terms[t + 2] for t in range(2)]
    return terms[0] + signs[0] * terms[1]


def cancel_kernel(shape, turn, place, index, *refs):
    blocks, rows, inner, tile = shape
    fields, refs = refs[:blocks], refs[blocks:]
    first, second, scale, coefs = refs[:4]
    out, s_one, s_two, r_one, r_two, ready, sent = refs[-11:-4]
    spare = itertools.cycle(refs[-4:])
    margin = (rows - inner) // 2
    width = first.shape[1] // 2
    chunk = 16
    mine = place[place.shape[0] - 1]
    skip = pl.multiple_of(mine * tile, chunk)
    dot = functools.partial(jnp.dot, preferred_element_type=jnp.float32)

    def tiles(value):
        return value.reshape(chunk // 8, 8, LANES)

    def gaps_at(block, start, rest=None, row=0, height=0):
        parts = []
        for part in range(2):
            value = fields[block][part, pl.ds(skip + start, chunk), :].astype(jnp.float32)
            if rest is not None:
                value = value - rest[block, pl.ds(part * height + row, chunk), :]
            parts.append(tiles(value))
        step, shift = (tiles(scale[i, pl.ds(start, chunk), :]) for i in range(2))
        return bit_gaps(*parts, step, shift, index, next(spare))

    def soften(block, out_ref, row, gaps):
        signs = [jnp.tanh(gap) for gap in gaps]
        for part in range(2):
            value = expand(signs, coefs, 16 * part).reshape(chunk, LANES)
            out_ref[block, pl.ds(part * width + row, chunk), :] = value.astype(jnp.bfloat16)

    def over(height, body, wanted=tuple(range(blocks))):
        parts = math.gcd(height // chunk, 4 // len(wanted))

        def step(i, carry):
            for part in range(parts):
                row = pl.multiple_of((parts * i + part) * chunk, chunk)
                for block in wanted:
                    body(block, row)
            return carry

        lax.fori_loop(0, height // (parts * chunk), step, 0)

    for ref, used_rows in ((s_one, rows), (s_two, inner)):
        if used_rows < width:
            blank = jnp.zeros((width - used_rows, LANES), jnp.bfloat16)
            for block in range(blocks):
                ref[block, used_rows:width, :] = blank
                ref[block, width + used_rows :, :] = blank

    def first_round(block, row):
        soften(block, s_one, row, gaps_at(block, row))

    def second_round(block, row):
        soften(block, s_two, row, gaps_at(block, row + margin, r_one, row, inner))

    def metrics(block, row):
        gaps = gaps_at(block, row + 2 * margin, r_two, row, tile)
        for bit in range(4):
            value = (gaps[bit] * 2.0).reshape(chunk, LANES)
            ready[block, bit, pl.ds(row, chunk), :] = value.astype(jnp.bfloat16)

    def send(block):
        lane = pl.multiple_of(place[blocks * turn + block] * LANES, LANES)
        target = out.at[:, :, pl.ds(lane, LANES)]
        return pltpu.make_async_copy(ready.at[block], target, sent.at[block])

    def product(matrix, ref, into):
        both = jnp.concatenate([ref[block] for block in range(blocks)], axis=1)
        result = dot(matrix[...], both)
        for block in range(blocks):
            into[block] = result[:, block * LANES : (block + 1) * LANES]

    over(rows, first_round)
    product(first, s_one, r_one)
    over(inner, second_round)
    product(second, s_two, r_two)
    for block in range(blocks):
        over(tile, metrics, (block,))
        send(block).start()
    for block in range(blocks):
        send(block).wait()


def cancel(turn, place, index, fields, first, second, scale, coefs, elements, before):
    samples = fields[0].shape[2]
    rows, inner, tile = scale.shape[1], first.shape[0] // 2, second.shape[0] // 2
    blocks = len(fields)
    vmem, smem = (pl.BlockSpec(memory_space=m) for m in (pltpu.VMEM, pltpu.SMEM))
    anywhere = pl.BlockSpec(memory_space=pl.ANY)
    given = [] if before is None else [before]
    wide = blocks * samples
    return pl.pallas_call(
        functools.partial(cancel_kernel, (blocks, rows, inner, tile), turn),
        in_specs=[smem] * 2 + [vmem] * (blocks + 4) + [anywhere] * len(given),
        out_specs=anywhere,
        scratch_shapes=[
            pltpu.VMEM((blocks, first.shape[1], samples), jnp.bfloat16),
            pltpu.VMEM((blocks, second.shape[1], samples), jnp.bfloat16),
            pltpu.VMEM((blocks, 2 * inner, samples), jnp.float32),
            pltpu.VMEM((blocks, 2 * tile, samples), jnp.float32),
            pltpu.VMEM((blocks, 4, tile, samples), jnp.bfloat16),
            pltpu.SemaphoreType.DMA((blocks,)),
        ]
        + [pltpu.VMEM((8, 2, 8, LANES), jnp.float32)] * 4,
        out_shape=jax.ShapeDtypeStruct((4, tile, elements), jnp.bfloat16),
        input_output_aliases={6 + blocks: 0} if given else {},
        compiler_params=pltpu.CompilerParams(vmem_limit_bytes=12 * MEBI),
        cost_estimate=pl.CostEstimate(
            flops=130 * (rows + inner + tile) * wide + 8 * inner * rows * wide,
            bytes_accessed=4 * rows * wide + 8 * tile * wide,
            transcendentals=4 * (rows + inner) * wide,
        ),
        name="cancel",
    )(place, index, *fields, first, second, scale, coefs, *given)


class Places:
    def __init__(self, mesh):
        self.tm, self.beam = mesh.shape["tm"], mesh.shape["beam"]
        self.square = self.tm == 4 and self.beam == 8

    def flat(self, y, x, z, core):
        return (y * 2 + x) * self.beam + z * 2 + core

    def swap(self, value, y=0, x=0, z=0, core=0):
        mask = self.flat(y, x, z, core)
        pairs = [(i, i ^ mask) for i in range(self.tm * self.beam)]
        return lax.ppermute(value, ("tm", "beam"), pairs)


def after(value, *others):
    return lax.optimization_barrier((value, *others))[0]


MASKS = [(y, x, z, core) for z in (0, 2) for y in range(2) for x in range(2) for core in range(2)]


def rows_held(places, rows):
    if not places.square:
        return jnp.arange(places.tm * places.beam * rows, dtype=jnp.int32)
    masks = [places.flat(y, x, z ^ near, core) for near in (0, 1) for y, x, z, core in MASKS]
    me = lax.axis_index("tm") * places.beam + lax.axis_index("beam")
    source = me ^ np.array(masks, np.int32)
    held = source[:, None] * rows + jnp.arange(rows, dtype=jnp.int32)[None, :]
    return held.reshape(-1)


def all_beams(places, element_signals, beam_weights, ready):
    if not places.square:
        gathered = lax.all_gather(beam_weights, ("tm", "beam"), axis=1, tiled=True)
        return form_beams([gathered], element_signals), None
    swap, w = places.swap, beam_weights
    w_z, w_x, w_y = swap(w, z=2), swap(w, x=1), swap(w, y=1)
    far = swap(after(element_signals, ready[2]), z=1)
    w_xy = swap(after(w_x, w_y), y=1)
    w_xz, w_yz = swap(after(w_z, w_y, *ready), x=1), swap(after(w_z, w_y, *ready), y=1)
    w_c, w_xc = swap(after(w, w_z), core=1), swap(after(w_x, w_z), core=1)
    w_yc, w_zc = swap(after(w_y, w_xy), core=1), swap(after(w_z, w_xy), core=1)
    w_xyc = swap(after(w_xy, w_zc), core=1)
    w_xyz = swap(after(w_yz, w_xz), x=1)
    w_xzc = swap(after(w_xz, w_xyc), core=1)
    w_yzc = swap(after(w_yz, w_xyc), core=1)
    w_xyzc = swap(w_xyz, core=1)
    pieces = [w, w_c, w_x, w_xc, w_y, w_yc, w_xy, w_xyc]
    pieces += [w_z, w_zc, w_xz, w_xzc, w_yz, w_yzc, w_xyz, w_xyzc]
    mine = form_beams(pieces, element_signals)
    other = form_beams(pieces, after(far, mine))
    return mine, other


def tables_kernel(shape, labels, taken, own, index, coefs, first, second, scale):
    slots, rows, inner, tile = shape
    margin = (rows - inner) // 2
    term = lax.broadcasted_iota(jnp.int32, (16, LANES), 0)
    sums = [jnp.zeros((16, LANES), jnp.float32) for _ in range(2)]
    for point in range(16):
        label = labels[point]
        index[label] = point // 4
        index[16 + label] = 4 + point % 4
        odd = term & label
        odd = odd ^ (odd >> 2)
        odd = (odd ^ (odd >> 1)) & 1
        sign = (1 - 2 * odd).astype(jnp.float32)
        for axis, step in ((0, point // 4), (1, point % 4)):
            sums[axis] += sign * ((2 * step - 3) * LEVEL / 16.0)
    for axis in range(2):
        for t in range(16):
            coefs[axis * 16 + t] = jnp.broadcast_to(sums[axis][t : t + 1, :], (8, LANES))
    half = jnp.broadcast_to(0.5 / taken[:, 3 * slots : 3 * slots + 1], scale.shape[1:])
    scale[0] = half * (2.0 * LEVEL)
    scale[1] = half * (8.0 * LEVEL * LEVEL)

    def matrix(out, skip, height, which):
        beams = jnp.broadcast_to(own[which : which + 1, :], (height, own.shape[1]))
        real = jnp.zeros(beams.shape, jnp.float32)
        imag = jnp.zeros(beams.shape, jnp.float32)
        for k in range(slots):
            near, r, i = (
                taken[skip : skip + height, g * slots + k : g * slots + k + 1] for g in range(3)
            )
            hit = near == beams
            real += jnp.where(hit, r, 0.0)
            imag += jnp.where(hit, i, 0.0)
        width = own.shape[1]
        out[:height, :width] = real.astype(jnp.bfloat16)
        out[:height, width:] = (-imag).astype(jnp.bfloat16)
        out[height:, :width] = imag.astype(jnp.bfloat16)
        out[height:, width:] = real.astype(jnp.bfloat16)

    matrix(first, margin, inner, 0)
    matrix(second, 2 * margin, tile, 1)


def tables(bit_labels, taken, own, slots, tile):
    rows, width = taken.shape[0], own.shape[1]
    inner = rows - 2 * COLS
    vmem, smem = (pl.BlockSpec(memory_space=m) for m in (pltpu.VMEM, pltpu.SMEM))
    return pl.pallas_call(
        functools.partial(tables_kernel, (slots, rows, inner, tile)),
        in_specs=[smem, vmem, vmem],
        out_specs=[smem, vmem, vmem, vmem, vmem],
        out_shape=[
            jax.ShapeDtypeStruct((32,), jnp.int32),
            jax.ShapeDtypeStruct((32, 8, LANES), jnp.float32),
            jax.ShapeDtypeStruct((2 * inner, 2 * width), jnp.bfloat16),
            jax.ShapeDtypeStruct((2 * tile, 2 * width), jnp.bfloat16),
            jax.ShapeDtypeStruct((2, rows, LANES), jnp.float32),
        ],
        compiler_params=pltpu.CompilerParams(vmem_limit_bytes=12 * MEBI),
        cost_estimate=pl.CostEstimate(
            flops=60 * rows * width, bytes_accessed=16 * rows * width, transcendentals=0
        ),
        name="tables",
    )(bit_labels, taken, own)


def on_device(places, element_signals, beam_weights, beam_order, neighbours, leakage, noise_var, bit_labels):
    count = beam_order.shape[0]
    tile = count // places.beam
    rows = tile + 2 * HALO
    slots = neighbours.shape[1]
    width = -(-rows // LANES) * LANES
    padded = jnp.pad(beam_order, (HALO, width + COLS), constant_values=-1)
    group = 2 if places.square else 1
    reach = group * tile
    span = reach + 2 * HALO
    windows = [padded[i : i + count : 1] for i in range(0, span, reach)]
    windows = jnp.concatenate([v.reshape(-1, reach) for v in windows], axis=1)[:, :span]
    own = lax.dynamic_slice_in_dim(padded, lax.axis_index("beam") * tile, width + COLS)
    sides = jnp.stack([own[:width], own[COLS:]]).astype(jnp.float32)
    table = jnp.concatenate(
        [
            neighbours.astype(jnp.float32),
            leakage[0].astype(jnp.float32),
            leakage[1].astype(jnp.float32),
            noise_var[:, None],
        ],
        axis=1,
    )
    taken = jnp.take(table, own[:rows], axis=0, mode="clip")
    held = rows_held(places, beam_weights.shape[1])
    me = lax.axis_index("beam")
    chips = places.beam // 2
    moves = (0, 1, 2, 3)
    if places.square:
        windows = windows[(me // 2) ^ np.array(moves, np.int32)]
    select = (windows[:, :, None] == held[None, None, :]).astype(jnp.bfloat16)
    mine, other = all_beams(places, element_signals, beam_weights, (select, taken, sides))
    beams = [mine]
    if other is not None:
        beams.append(places.swap(other, z=1))
        taken = after(taken, other)
    index, coefs, first, second, scale = tables(bit_labels, taken, sides, slots, tile)
    select = after(select, first, second, scale, coefs)
    ordered = list(order_beams(select, beams))
    elements = element_signals.shape[2] * places.beam
    if places.square:
        here, one, two, three = ordered
        one = places.swap(one, z=1)
        shifts = np.array([0, 0, 1, 2, 1, 2, 3, 3], np.int32)
        flips = np.array([0, 1, 0, 0, 1, 1, 0, 1], np.int32)
        place = me ^ (2 * shifts + flips)
        place = jnp.concatenate([place, (me % 2)[None]])
    else:
        fields = list(
            lax.all_to_all(jnp.stack(ordered), "beam", split_axis=0, concat_axis=0, tiled=True)
        )
        pairs = [fields[2 * i : 2 * i + 2] for i in range(chips)]
        place = jnp.arange(places.beam + 1, dtype=jnp.int32) % places.beam

    def run(turn, pair, before):
        return cancel(turn, place, index, pair, first, second, scale, coefs, elements, before)

    if places.square:
        two = places.swap(two, z=2)
        out = run(0, [here, places.swap(here, core=1)], None)
        three = places.swap(after(three, out), z=3)
        one, two = after(one, out), after(two, out)
        far_one, far_two = places.swap(one, core=1), places.swap(two, core=1)
        out = run(1, [one, two], out)
        out = run(2, [far_one, far_two], out)
        three = after(three, out)
        return run(3, [three, places.swap(three, core=1)], out)
    out = None
    for i in range(chips):
        out = run(i, pairs[i], out)
    return out


def solution(mesh):
    in_specs = (
        P(None, None, ("tm", "beam")),
        P(None, ("tm", "beam"), None),
        P(),
        P(),
        P(),
        P(),
        P(),
    )
    return jax.shard_map(
        functools.partial(on_device, Places(mesh)),
        mesh=mesh,
        in_specs=in_specs,
        out_specs=P(None, "beam", "tm"),
        check_vma=False,
    )
```

```python
import functools
import itertools
import math

import jax
import jax.numpy as jnp
import numpy as np
from jax import lax
from jax.experimental import pallas as pl
from jax.experimental.pallas import tpu as pltpu
from jax.sharding import PartitionSpec as P

COLS = 16
HALO = 2 * COLS
LEVEL = 0.31622776601683794
LANES = 128
MEBI = 1 << 20


def beams_kernel(pieces, *refs):
    weights, signals, out, total = refs[:pieces], *refs[pieces:]
    elements = weights[0].shape[2]
    depth = math.gcd(elements, 512)
    for start in range(0, elements, depth):
        part = slice(start, start + depth)
        stack = jnp.concatenate(
            [w[0, :, part] for w in weights] + [w[1, :, part] for w in weights], axis=0
        )
        wide = jnp.concatenate([signals[0, part, :], signals[1, part, :]], axis=1)
        product = jnp.dot(stack, wide, preferred_element_type=jnp.float32)
        if start:
            total[...] += product
        else:
            total[...] = product
    rows, samples = total.shape[0] // 2, signals.shape[2]
    out[0] = (total[:rows, :samples] - total[rows:, samples:]).astype(jnp.bfloat16)
    out[1] = (total[:rows, samples:] + total[rows:, :samples]).astype(jnp.bfloat16)


def form_beams(weights, signals):
    pieces = len(weights)
    rows, elements = weights[0].shape[1:]
    samples = signals.shape[2]
    all_rows = pieces * rows
    whole = pl.BlockSpec(memory_space=pltpu.VMEM)
    return pl.pallas_call(
        functools.partial(beams_kernel, pieces),
        in_specs=[whole] * (pieces + 1),
        out_specs=whole,
        out_shape=jax.ShapeDtypeStruct((2, all_rows, samples), jnp.bfloat16),
        scratch_shapes=[pltpu.VMEM((2 * all_rows, 2 * samples), jnp.float32)],
        compiler_params=pltpu.CompilerParams(vmem_limit_bytes=12 * MEBI),
        cost_estimate=pl.CostEstimate(
            flops=8 * all_rows * elements * samples,
            bytes_accessed=4 * elements * (all_rows + samples),
            transcendentals=0,
        ),
        name="form_beams",
    )(*weights, signals)


def order_kernel(parts, *refs):
    select, beams, outs = refs[0], refs[1 : 1 + parts], refs[1 + parts :]
    real = jnp.concatenate([b[0] for b in beams], axis=0)
    imag = jnp.concatenate([b[1] for b in beams], axis=0)
    both = jnp.concatenate([real, imag], axis=1)
    samples = real.shape[1]
    for d, out in enumerate(outs):
        picked = jnp.dot(select[d], both, preferred_element_type=jnp.float32)
        out[0] = picked[:, :samples].astype(jnp.bfloat16)
        out[1] = picked[:, samples:].astype(jnp.bfloat16)


def order_beams(select, beams):
    tiles, rows, count = select.shape
    samples = beams[0].shape[2]
    whole = pl.BlockSpec(memory_space=pltpu.VMEM)
    return pl.pallas_call(
        functools.partial(order_kernel, len(beams)),
        in_specs=[whole] * (1 + len(beams)),
        out_specs=[whole] * tiles,
        out_shape=[jax.ShapeDtypeStruct((2, rows, samples), jnp.bfloat16)] * tiles,
        compiler_params=pltpu.CompilerParams(vmem_limit_bytes=12 * MEBI),
        cost_estimate=pl.CostEstimate(
            flops=4 * tiles * rows * count * samples,
            bytes_accessed=2 * tiles * rows * (count + 2 * samples),
            transcendentals=0,
        ),
        name="order_beams",
    )(select, *beams)


def bit_gaps(real, imag, step, shift, index, scratch):
    for axis, field in ((0, real), (1, imag)):
        near = field * step
        triple = near * 3.0
        scratch[axis * 4] = shift + triple
        scratch[axis * 4 + 1] = near
        scratch[axis * 4 + 2] = -near
        scratch[axis * 4 + 3] = shift - triple
    far = [scratch[index[label]] + scratch[index[16 + label]] for label in range(16)]
    least = jnp.minimum
    low = [
        least(least(far[b], far[b + 4]), least(far[b + 8], far[b + 12])) for b in range(4)
    ]
    high = [
        least(least(far[4 * b], far[4 * b + 1]), least(far[4 * b + 2], far[4 * b + 3]))
        for b in range(4)
    ]
    gaps = []
    for part in (low, high):
        gaps.append(least(part[1], part[3]) - least(part[0], part[2]))
        gaps.append(least(part[2], part[3]) - least(part[0], part[1]))
    return gaps


def expand(signs, coefs, base):
    terms = [coefs[base + t] + signs[3] * coefs[base + t + 8] for t in range(8)]
    terms = [terms[t] + signs[2] * terms[t + 4] for t in range(4)]
    terms = [terms[t] + signs[1] * terms[t + 2] for t in range(2)]
    return terms[0] + signs[0] * terms[1]


def cancel_kernel(shape, turn, place, index, *refs):
    blocks, rows, inner, tile = shape
    fields, refs = refs[:blocks], refs[blocks:]
    first, second, scale, coefs = refs[:4]
    out, s_one, s_two, r_one, r_two, ready, sent = refs[-11:-4]
    spare = itertools.cycle(refs[-4:])
    margin = (rows - inner) // 2
    width = first.shape[1] // 2
    chunk = 16
    mine = place[place.shape[0] - 1]
    skip = pl.multiple_of(mine * tile, chunk)
    dot = functools.partial(jnp.dot, preferred_element_type=jnp.float32)

    def tiles(value):
        return value.reshape(chunk // 8, 8, LANES)

    def gaps_at(block, start, rest=None, row=0, height=0):
        parts = []
        for part in range(2):
            value = fields[block][part, pl.ds(skip + start, chunk), :].astype(jnp.float32)
            if rest is not None:
                value = value - rest[block, pl.ds(part * height + row, chunk), :]
            parts.append(tiles(value))
        step, shift = (tiles(scale[i, pl.ds(start, chunk), :]) for i in range(2))
        return bit_gaps(*parts, step, shift, index, next(spare))

    def soften(block, out_ref, row, gaps):
        signs = [jnp.tanh(gap) for gap in gaps]
        for part in range(2):
            value = expand(signs, coefs, 16 * part).reshape(chunk, LANES)
            out_ref[block, pl.ds(part * width + row, chunk), :] = value.astype(jnp.bfloat16)

    def over(height, body, wanted=tuple(range(blocks))):
        parts = math.gcd(height // chunk, 4 // len(wanted))

        def step(i, carry):
            for part in range(parts):
                row = pl.multiple_of((parts * i + part) * chunk, chunk)
                for block in wanted:
                    body(block, row)
            return carry

        lax.fori_loop(0, height // (parts * chunk), step, 0)

    for ref, used_rows in ((s_one, rows), (s_two, inner)):
        if used_rows < width:
            blank = jnp.zeros((width - used_rows, LANES), jnp.bfloat16)
            for block in range(blocks):
                ref[block, used_rows:width, :] = blank
                ref[block, width + used_rows :, :] = blank

    def first_round(block, row):
        soften(block, s_one, row, gaps_at(block, row))

    def second_round(block, row):
        soften(block, s_two, row, gaps_at(block, row + margin, r_one, row, inner))

    def metrics(block, row):
        gaps = gaps_at(block, row + 2 * margin, r_two, row, tile)
        for bit in range(4):
            value = (gaps[bit] * 2.0).reshape(chunk, LANES)
            ready[block, bit, pl.ds(row, chunk), :] = value.astype(jnp.bfloat16)

    def send(block):
        lane = pl.multiple_of(place[blocks * turn + block] * LANES, LANES)
        target = out.at[:, :, pl.ds(lane, LANES)]
        return pltpu.make_async_copy(ready.at[block], target, sent.at[block])

    def product(matrix, ref, into):
        both = jnp.concatenate([ref[block] for block in range(blocks)], axis=1)
        result = dot(matrix[...], both)
        for block in range(blocks):
            into[block] = result[:, block * LANES : (block + 1) * LANES]

    over(rows, first_round)
    product(first, s_one, r_one)
    over(inner, second_round)
    product(second, s_two, r_two)
    for block in range(blocks):
        over(tile, metrics, (block,))
        send(block).start()
    for block in range(blocks):
        send(block).wait()


def cancel(turn, place, index, fields, first, second, scale, coefs, elements, before):
    samples = fields[0].shape[2]
    rows, inner, tile = scale.shape[1], first.shape[0] // 2, second.shape[0] // 2
    blocks = len(fields)
    vmem, smem = (pl.BlockSpec(memory_space=m) for m in (pltpu.VMEM, pltpu.SMEM))
    anywhere = pl.BlockSpec(memory_space=pl.ANY)
    given = [] if before is None else [before]
    wide = blocks * samples
    return pl.pallas_call(
        functools.partial(cancel_kernel, (blocks, rows, inner, tile), turn),
        in_specs=[smem] * 2 + [vmem] * (blocks + 4) + [anywhere] * len(given),
        out_specs=anywhere,
        scratch_shapes=[
            pltpu.VMEM((blocks, first.shape[1], samples), jnp.bfloat16),
            pltpu.VMEM((blocks, second.shape[1], samples), jnp.bfloat16),
            pltpu.VMEM((blocks, 2 * inner, samples), jnp.float32),
            pltpu.VMEM((blocks, 2 * tile, samples), jnp.float32),
            pltpu.VMEM((blocks, 4, tile, samples), jnp.bfloat16),
            pltpu.SemaphoreType.DMA((blocks,)),
        ]
        + [pltpu.VMEM((8, 2, 8, LANES), jnp.float32)] * 4,
        out_shape=jax.ShapeDtypeStruct((4, tile, elements), jnp.bfloat16),
        input_output_aliases={6 + blocks: 0} if given else {},
        compiler_params=pltpu.CompilerParams(vmem_limit_bytes=12 * MEBI),
        cost_estimate=pl.CostEstimate(
            flops=130 * (rows + inner + tile) * wide + 8 * inner * rows * wide,
            bytes_accessed=4 * rows * wide + 8 * tile * wide,
            transcendentals=4 * (rows + inner) * wide,
        ),
        name="cancel",
    )(place, index, *fields, first, second, scale, coefs, *given)


class Places:
    def __init__(self, mesh):
        self.tm, self.beam = mesh.shape["tm"], mesh.shape["beam"]
        self.square = self.tm == 4 and self.beam == 8

    def flat(self, y, x, z, core):
        return (y * 2 + x) * self.beam + z * 2 + core

    def swap(self, value, y=0, x=0, z=0, core=0):
        mask = self.flat(y, x, z, core)
        pairs = [(i, i ^ mask) for i in range(self.tm * self.beam)]
        return lax.ppermute(value, ("tm", "beam"), pairs)


def after(value, *others):
    return lax.optimization_barrier((value, *others))[0]


MASKS = [(y, x, z, core) for z in (0, 2) for y in range(2) for x in range(2) for core in range(2)]


def rows_held(places, rows):
    if not places.square:
        return jnp.arange(places.tm * places.beam * rows, dtype=jnp.int32)
    masks = [places.flat(y, x, z ^ near, core) for near in (0, 1) for y, x, z, core in MASKS]
    me = lax.axis_index("tm") * places.beam + lax.axis_index("beam")
    source = me ^ np.array(masks, np.int32)
    held = source[:, None] * rows + jnp.arange(rows, dtype=jnp.int32)[None, :]
    return held.reshape(-1)


def all_beams(places, element_signals, beam_weights, ready):
    if not places.square:
        gathered = lax.all_gather(beam_weights, ("tm", "beam"), axis=1, tiled=True)
        return form_beams([gathered], element_signals), None
    swap, w = places.swap, beam_weights
    w_z, w_x, w_y = swap(w, z=2), swap(w, x=1), swap(w, y=1)
    far = swap(after(element_signals, ready[2]), z=1)
    w_xy = swap(after(w_x, w_y), y=1)
    w_xz, w_yz = swap(after(w_z, w_y, *ready), x=1), swap(after(w_z, w_y, *ready), y=1)
    w_c, w_xc = swap(after(w, w_z), core=1), swap(after(w_x, w_z), core=1)
    w_yc, w_zc = swap(after(w_y, w_xy), core=1), swap(after(w_z, w_xy), core=1)
    w_xyc = swap(after(w_xy, w_zc), core=1)
    w_xyz = swap(after(w_yz, w_xz), x=1)
    w_xzc = swap(after(w_xz, w_xyc), core=1)
    w_yzc = swap(after(w_yz, w_xyc), core=1)
    w_xyzc = swap(w_xyz, core=1)
    pieces = [w, w_c, w_x, w_xc, w_y, w_yc, w_xy, w_xyc]
    pieces += [w_z, w_zc, w_xz, w_xzc, w_yz, w_yzc, w_xyz, w_xyzc]
    mine = form_beams(pieces, element_signals)
    other = form_beams(pieces, after(far, mine))
    return mine, other


def tables_kernel(shape, labels, taken, own, index, coefs, first, second, scale):
    slots, rows, inner, tile = shape
    margin = (rows - inner) // 2
    term = lax.broadcasted_iota(jnp.int32, (16, LANES), 0)
    sums = [jnp.zeros((16, LANES), jnp.float32) for _ in range(2)]
    for point in range(16):
        label = labels[point]
        index[label] = point // 4
        index[16 + label] = 4 + point % 4
        odd = term & label
        odd = odd ^ (odd >> 2)
        odd = (odd ^ (odd >> 1)) & 1
        sign = (1 - 2 * odd).astype(jnp.float32)
        for axis, step in ((0, point // 4), (1, point % 4)):
            sums[axis] += sign * ((2 * step - 3) * LEVEL / 16.0)
    for axis in range(2):
        for t in range(16):
            coefs[axis * 16 + t] = jnp.broadcast_to(sums[axis][t : t + 1, :], (8, LANES))
    half = jnp.broadcast_to(0.5 / taken[:, 3 * slots : 3 * slots + 1], scale.shape[1:])
    scale[0] = half * (2.0 * LEVEL)
    scale[1] = half * (8.0 * LEVEL * LEVEL)

    def matrix(out, skip, height, which):
        beams = jnp.broadcast_to(own[which : which + 1, :], (height, own.shape[1]))
        real = jnp.zeros(beams.shape, jnp.float32)
        imag = jnp.zeros(beams.shape, jnp.float32)
        for k in range(slots):
            near, r, i = (
                taken[skip : skip + height, g * slots + k : g * slots + k + 1] for g in range(3)
            )
            hit = near == beams
            real += jnp.where(hit, r, 0.0)
            imag += jnp.where(hit, i, 0.0)
        width = own.shape[1]
        out[:height, :width] = real.astype(jnp.bfloat16)
        out[:height, width:] = (-imag).astype(jnp.bfloat16)
        out[height:, :width] = imag.astype(jnp.bfloat16)
        out[height:, width:] = real.astype(jnp.bfloat16)

    matrix(first, margin, inner, 0)
    matrix(second, 2 * margin, tile, 1)


def tables(bit_labels, taken, own, slots, tile):
    rows, width = taken.shape[0], own.shape[1]
    inner = rows - 2 * COLS
    vmem, smem = (pl.BlockSpec(memory_space=m) for m in (pltpu.VMEM, pltpu.SMEM))
    return pl.pallas_call(
        functools.partial(tables_kernel, (slots, rows, inner, tile)),
        in_specs=[smem, vmem, vmem],
        out_specs=[smem, vmem, vmem, vmem, vmem],
        out_shape=[
            jax.ShapeDtypeStruct((32,), jnp.int32),
            jax.ShapeDtypeStruct((32, 8, LANES), jnp.float32),
            jax.ShapeDtypeStruct((2 * inner, 2 * width), jnp.bfloat16),
            jax.ShapeDtypeStruct((2 * tile, 2 * width), jnp.bfloat16),
            jax.ShapeDtypeStruct((2, rows, LANES), jnp.float32),
        ],
        compiler_params=pltpu.CompilerParams(vmem_limit_bytes=12 * MEBI),
        cost_estimate=pl.CostEstimate(
            flops=60 * rows * width, bytes_accessed=16 * rows * width, transcendentals=0
        ),
        name="tables",
    )(bit_labels, taken, own)


def on_device(places, element_signals, beam_weights, beam_order, neighbours, leakage, noise_var, bit_labels):
    count = beam_order.shape[0]
    tile = count // places.beam
    rows = tile + 2 * HALO
    slots = neighbours.shape[1]
    width = -(-rows // LANES) * LANES
    padded = jnp.pad(beam_order, (HALO, width + COLS), constant_values=-1)
    group = 2 if places.square else 1
    reach = group * tile
    span = reach + 2 * HALO
    windows = [padded[i : i + count : 1] for i in range(0, span, reach)]
    windows = jnp.concatenate([v.reshape(-1, reach) for v in windows], axis=1)[:, :span]
    own = lax.dynamic_slice_in_dim(padded, lax.axis_index("beam") * tile, width + COLS)
    sides = jnp.stack([own[:width], own[COLS:]]).astype(jnp.float32)
    table = jnp.concatenate(
        [
            neighbours.astype(jnp.float32),
            leakage[0].astype(jnp.float32),
            leakage[1].astype(jnp.float32),
            noise_var[:, None],
        ],
        axis=1,
    )
    taken = jnp.take(table, own[:rows], axis=0, mode="clip")
    held = rows_held(places, beam_weights.shape[1])
    me = lax.axis_index("beam")
    chips = places.beam // 2
    moves = (0, 1, 2, 3)
    if places.square:
        windows = windows[(me // 2) ^ np.array(moves, np.int32)]
    select = (windows[:, :, None] == held[None, None, :]).astype(jnp.bfloat16)
    mine, other = all_beams(places, element_signals, beam_weights, (select, taken, sides))
    beams = [mine]
    if other is not None:
        beams.append(places.swap(other, z=1))
        taken = after(taken, other)
    index, coefs, first, second, scale = tables(bit_labels, taken, sides, slots, tile)
    select = after(select, first, second, scale, coefs)
    ordered = list(order_beams(select, beams))
    elements = element_signals.shape[2] * places.beam
    if places.square:
        here, one, two, three = ordered
        one = places.swap(one, z=1)
        shifts = np.array([0, 0, 1, 2, 1, 2, 3, 3], np.int32)
        flips = np.array([0, 1, 0, 0, 1, 1, 0, 1], np.int32)
        place = me ^ (2 * shifts + flips)
        place = jnp.concatenate([place, (me % 2)[None]])
    else:
        fields = list(
            lax.all_to_all(jnp.stack(ordered), "beam", split_axis=0, concat_axis=0, tiled=True)
        )
        pairs = [fields[2 * i : 2 * i + 2] for i in range(chips)]
        place = jnp.arange(places.beam + 1, dtype=jnp.int32) % places.beam

    def run(turn, pair, before):
        return cancel(turn, place, index, pair, first, second, scale, coefs, elements, before)

    if places.square:
        two = places.swap(two, z=2)
        out = run(0, [here, places.swap(here, core=1)], None)
        one, two = after(one, out), after(two, out)
        three = places.swap(after(three, two), z=3)
        far_one, far_two = places.swap(one, core=1), places.swap(two, core=1)
        out = run(1, [one, two], out)
        out = run(2, [far_one, far_two], out)
        three = after(three, out)
        return run(3, [three, places.swap(three, core=1)], out)
    out = None
    for i in range(chips):
        out = run(i, pairs[i], out)
    return out


def solution(mesh):
    in_specs = (
        P(None, None, ("tm", "beam")),
        P(None, ("tm", "beam"), None),
        P(),
        P(),
        P(),
        P(),
        P(),
    )
    return jax.shard_map(
        functools.partial(on_device, Places(mesh)),
        mesh=mesh,
        in_specs=in_specs,
        out_specs=P(None, "beam", "tm"),
        check_vma=False,
    )
```

```python
import functools
import itertools
import math

import jax
import jax.numpy as jnp
import numpy as np
from jax import lax
from jax.experimental import pallas as pl
from jax.experimental.pallas import tpu as pltpu
from jax.sharding import PartitionSpec as P

COLS = 16
HALO = 2 * COLS
LEVEL = 0.31622776601683794
LANES = 128
MEBI = 1 << 20


def beams_kernel(pieces, *refs):
    weights, signals, out, total = refs[:pieces], *refs[pieces:]
    elements = weights[0].shape[2]
    depth = math.gcd(elements, 512)
    for start in range(0, elements, depth):
        part = slice(start, start + depth)
        stack = jnp.concatenate(
            [w[0, :, part] for w in weights] + [w[1, :, part] for w in weights], axis=0
        )
        wide = jnp.concatenate([signals[0, part, :], signals[1, part, :]], axis=1)
        product = jnp.dot(stack, wide, preferred_element_type=jnp.float32)
        if start:
            total[...] += product
        else:
            total[...] = product
    rows, samples = total.shape[0] // 2, signals.shape[2]
    out[0] = (total[:rows, :samples] - total[rows:, samples:]).astype(jnp.bfloat16)
    out[1] = (total[:rows, samples:] + total[rows:, :samples]).astype(jnp.bfloat16)


def form_beams(weights, signals):
    pieces = len(weights)
    rows, elements = weights[0].shape[1:]
    samples = signals.shape[2]
    all_rows = pieces * rows
    whole = pl.BlockSpec(memory_space=pltpu.VMEM)
    return pl.pallas_call(
        functools.partial(beams_kernel, pieces),
        in_specs=[whole] * (pieces + 1),
        out_specs=whole,
        out_shape=jax.ShapeDtypeStruct((2, all_rows, samples), jnp.bfloat16),
        scratch_shapes=[pltpu.VMEM((2 * all_rows, 2 * samples), jnp.float32)],
        compiler_params=pltpu.CompilerParams(vmem_limit_bytes=12 * MEBI),
        cost_estimate=pl.CostEstimate(
            flops=8 * all_rows * elements * samples,
            bytes_accessed=4 * elements * (all_rows + samples),
            transcendentals=0,
        ),
        name="form_beams",
    )(*weights, signals)


def order_kernel(parts, *refs):
    select, beams, outs = refs[0], refs[1 : 1 + parts], refs[1 + parts :]
    real = jnp.concatenate([b[0] for b in beams], axis=0)
    imag = jnp.concatenate([b[1] for b in beams], axis=0)
    both = jnp.concatenate([real, imag], axis=1)
    samples = real.shape[1]
    for d, out in enumerate(outs):
        picked = jnp.dot(select[d], both, preferred_element_type=jnp.float32)
        out[0] = picked[:, :samples].astype(jnp.bfloat16)
        out[1] = picked[:, samples:].astype(jnp.bfloat16)


def order_beams(select, beams):
    tiles, rows, count = select.shape
    samples = beams[0].shape[2]
    whole = pl.BlockSpec(memory_space=pltpu.VMEM)
    return pl.pallas_call(
        functools.partial(order_kernel, len(beams)),
        in_specs=[whole] * (1 + len(beams)),
        out_specs=[whole] * tiles,
        out_shape=[jax.ShapeDtypeStruct((2, rows, samples), jnp.bfloat16)] * tiles,
        compiler_params=pltpu.CompilerParams(vmem_limit_bytes=12 * MEBI),
        cost_estimate=pl.CostEstimate(
            flops=4 * tiles * rows * count * samples,
            bytes_accessed=2 * tiles * rows * (count + 2 * samples),
            transcendentals=0,
        ),
        name="order_beams",
    )(select, *beams)


def bit_gaps(real, imag, step, shift, index, scratch):
    for axis, field in ((0, real), (1, imag)):
        near = field * step
        triple = near * 3.0
        scratch[axis * 4] = shift + triple
        scratch[axis * 4 + 1] = near
        scratch[axis * 4 + 2] = -near
        scratch[axis * 4 + 3] = shift - triple
    far = [scratch[index[label]] + scratch[index[16 + label]] for label in range(16)]
    least = jnp.minimum
    low = [
        least(least(far[b], far[b + 4]), least(far[b + 8], far[b + 12])) for b in range(4)
    ]
    high = [
        least(least(far[4 * b], far[4 * b + 1]), least(far[4 * b + 2], far[4 * b + 3]))
        for b in range(4)
    ]
    gaps = []
    for part in (low, high):
        gaps.append(least(part[1], part[3]) - least(part[0], part[2]))
        gaps.append(least(part[2], part[3]) - least(part[0], part[1]))
    return gaps


def expand(signs, coefs, base):
    terms = [coefs[base + t] + signs[3] * coefs[base + t + 8] for t in range(8)]
    terms = [terms[t] + signs[2] * terms[t + 4] for t in range(4)]
    terms = [terms[t] + signs[1] * terms[t + 2] for t in range(2)]
    return terms[0] + signs[0] * terms[1]


def cancel_kernel(shape, turn, place, index, *refs):
    blocks, rows, inner, tile = shape
    fields, refs = refs[:blocks], refs[blocks:]
    first, second, scale, coefs = refs[:4]
    out, s_one, s_two, r_one, r_two, ready, sent = refs[-11:-4]
    spare = itertools.cycle(refs[-4:])
    margin = (rows - inner) // 2
    width = first.shape[1] // 2
    chunk = 16
    mine = place[place.shape[0] - 1]
    skip = pl.multiple_of(mine * tile, chunk)
    dot = functools.partial(jnp.dot, preferred_element_type=jnp.float32)

    def tiles(value):
        return value.reshape(chunk // 8, 8, LANES)

    def gaps_at(block, start, rest=None, row=0, height=0):
        parts = []
        for part in range(2):
            value = fields[block][part, pl.ds(skip + start, chunk), :].astype(jnp.float32)
            if rest is not None:
                value = value - rest[block, pl.ds(part * height + row, chunk), :]
            parts.append(tiles(value))
        step, shift = (tiles(scale[i, pl.ds(start, chunk), :]) for i in range(2))
        return bit_gaps(*parts, step, shift, index, next(spare))

    def soften(block, out_ref, row, gaps):
        signs = [jnp.tanh(gap) for gap in gaps]
        for part in range(2):
            value = expand(signs, coefs, 16 * part).reshape(chunk, LANES)
            out_ref[block, pl.ds(part * width + row, chunk), :] = value.astype(jnp.bfloat16)

    def over(height, body, wanted=tuple(range(blocks))):
        parts = math.gcd(height // chunk, 4 // len(wanted))

        def step(i, carry):
            for part in range(parts):
                row = pl.multiple_of((parts * i + part) * chunk, chunk)
                for block in wanted:
                    body(block, row)
            return carry

        lax.fori_loop(0, height // (parts * chunk), step, 0)

    for ref, used_rows in ((s_one, rows), (s_two, inner)):
        if used_rows < width:
            blank = jnp.zeros((width - used_rows, LANES), jnp.bfloat16)
            for block in range(blocks):
                ref[block, used_rows:width, :] = blank
                ref[block, width + used_rows :, :] = blank

    def first_round(block, row):
        soften(block, s_one, row, gaps_at(block, row))

    def second_round(block, row):
        soften(block, s_two, row, gaps_at(block, row + margin, r_one, row, inner))

    def metrics(block, row):
        gaps = gaps_at(block, row + 2 * margin, r_two, row, tile)
        for bit in range(4):
            value = (gaps[bit] * 2.0).reshape(chunk, LANES)
            ready[block, bit, pl.ds(row, chunk), :] = value.astype(jnp.bfloat16)

    def send(block):
        lane = pl.multiple_of(place[blocks * turn + block] * LANES, LANES)
        target = out.at[:, :, pl.ds(lane, LANES)]
        return pltpu.make_async_copy(ready.at[block], target, sent.at[block])

    def product(matrix, ref, into):
        both = jnp.concatenate([ref[block] for block in range(blocks)], axis=1)
        result = dot(matrix[...], both)
        for block in range(blocks):
            into[block] = result[:, block * LANES : (block + 1) * LANES]

    over(rows, first_round)
    product(first, s_one, r_one)
    over(inner, second_round)
    product(second, s_two, r_two)
    for block in range(blocks):
        over(tile, metrics, (block,))
        send(block).start()
    for block in range(blocks):
        send(block).wait()


def cancel(turn, place, index, fields, first, second, scale, coefs, elements, before):
    samples = fields[0].shape[2]
    rows, inner, tile = scale.shape[1], first.shape[0] // 2, second.shape[0] // 2
    blocks = len(fields)
    vmem, smem = (pl.BlockSpec(memory_space=m) for m in (pltpu.VMEM, pltpu.SMEM))
    anywhere = pl.BlockSpec(memory_space=pl.ANY)
    given = [] if before is None else [before]
    wide = blocks * samples
    return pl.pallas_call(
        functools.partial(cancel_kernel, (blocks, rows, inner, tile), turn),
        in_specs=[smem] * 2 + [vmem] * (blocks + 4) + [anywhere] * len(given),
        out_specs=anywhere,
        scratch_shapes=[
            pltpu.VMEM((blocks, first.shape[1], samples), jnp.bfloat16),
            pltpu.VMEM((blocks, second.shape[1], samples), jnp.bfloat16),
            pltpu.VMEM((blocks, 2 * inner, samples), jnp.float32),
            pltpu.VMEM((blocks, 2 * tile, samples), jnp.float32),
            pltpu.VMEM((blocks, 4, tile, samples), jnp.bfloat16),
            pltpu.SemaphoreType.DMA((blocks,)),
        ]
        + [pltpu.VMEM((8, 2, 8, LANES), jnp.float32)] * 4,
        out_shape=jax.ShapeDtypeStruct((4, tile, elements), jnp.bfloat16),
        input_output_aliases={6 + blocks: 0} if given else {},
        compiler_params=pltpu.CompilerParams(vmem_limit_bytes=12 * MEBI),
        cost_estimate=pl.CostEstimate(
            flops=130 * (rows + inner + tile) * wide + 8 * inner * rows * wide,
            bytes_accessed=4 * rows * wide + 8 * tile * wide,
            transcendentals=4 * (rows + inner) * wide,
        ),
        name="cancel",
    )(place, index, *fields, first, second, scale, coefs, *given)


class Places:
    def __init__(self, mesh):
        self.tm, self.beam = mesh.shape["tm"], mesh.shape["beam"]
        self.square = self.tm == 4 and self.beam == 8

    def flat(self, y, x, z, core):
        return (y * 2 + x) * self.beam + z * 2 + core

    def swap(self, value, y=0, x=0, z=0, core=0):
        mask = self.flat(y, x, z, core)
        pairs = [(i, i ^ mask) for i in range(self.tm * self.beam)]
        return lax.ppermute(value, ("tm", "beam"), pairs)


def after(value, *others):
    return lax.optimization_barrier((value, *others))[0]


MASKS = [(y, x, z, core) for z in (0, 2) for y in range(2) for x in range(2) for core in range(2)]


def rows_held(places, rows):
    if not places.square:
        return jnp.arange(places.tm * places.beam * rows, dtype=jnp.int32)
    masks = [places.flat(y, x, z ^ near, core) for near in (0, 1) for y, x, z, core in MASKS]
    me = lax.axis_index("tm") * places.beam + lax.axis_index("beam")
    source = me ^ np.array(masks, np.int32)
    held = source[:, None] * rows + jnp.arange(rows, dtype=jnp.int32)[None, :]
    return held.reshape(-1)


def all_beams(places, element_signals, beam_weights, ready):
    if not places.square:
        gathered = lax.all_gather(beam_weights, ("tm", "beam"), axis=1, tiled=True)
        return form_beams([gathered], element_signals), None
    swap, w = places.swap, beam_weights
    w_z, w_x, w_y = swap(w, z=2), swap(w, x=1), swap(w, y=1)
    far = swap(after(element_signals, ready[2]), z=1)
    w_xy = swap(after(w_x, w_y), y=1)
    w_xz, w_yz = swap(after(w_z, w_y, *ready), x=1), swap(after(w_z, w_y, *ready), y=1)
    w_c, w_xc = swap(after(w, w_z), core=1), swap(after(w_x, w_z), core=1)
    w_yc, w_zc = swap(after(w_y, w_xy), core=1), swap(after(w_z, w_xy), core=1)
    w_xyc = swap(after(w_xy, w_zc), core=1)
    w_xyz = swap(after(w_yz, w_xz), x=1)
    w_xzc = swap(after(w_xz, w_xyc), core=1)
    w_yzc = swap(after(w_yz, w_xyc), core=1)
    w_xyzc = swap(w_xyz, core=1)
    pieces = [w, w_c, w_x, w_xc, w_y, w_yc, w_xy, w_xyc]
    pieces += [w_z, w_zc, w_xz, w_xzc, w_yz, w_yzc, w_xyz, w_xyzc]
    early = form_beams(pieces[:8], far)
    mine = form_beams(pieces, after(element_signals, early))
    other = [early, form_beams(pieces[8:], after(far, mine))]
    return mine, other


def tables_kernel(shape, labels, taken, own, index, coefs, first, second, scale):
    slots, rows, inner, tile = shape
    margin = (rows - inner) // 2
    term = lax.broadcasted_iota(jnp.int32, (16, LANES), 0)
    sums = [jnp.zeros((16, LANES), jnp.float32) for _ in range(2)]
    for point in range(16):
        label = labels[point]
        index[label] = point // 4
        index[16 + label] = 4 + point % 4
        odd = term & label
        odd = odd ^ (odd >> 2)
        odd = (odd ^ (odd >> 1)) & 1
        sign = (1 - 2 * odd).astype(jnp.float32)
        for axis, step in ((0, point // 4), (1, point % 4)):
            sums[axis] += sign * ((2 * step - 3) * LEVEL / 16.0)
    for axis in range(2):
        for t in range(16):
            coefs[axis * 16 + t] = jnp.broadcast_to(sums[axis][t : t + 1, :], (8, LANES))
    half = jnp.broadcast_to(0.5 / taken[:, 3 * slots : 3 * slots + 1], scale.shape[1:])
    scale[0] = half * (2.0 * LEVEL)
    scale[1] = half * (8.0 * LEVEL * LEVEL)

    def matrix(out, skip, height, which):
        beams = jnp.broadcast_to(own[which : which + 1, :], (height, own.shape[1]))
        real = jnp.zeros(beams.shape, jnp.float32)
        imag = jnp.zeros(beams.shape, jnp.float32)
        for k in range(slots):
            near, r, i = (
                taken[skip : skip + height, g * slots + k : g * slots + k + 1] for g in range(3)
            )
            hit = near == beams
            real += jnp.where(hit, r, 0.0)
            imag += jnp.where(hit, i, 0.0)
        width = own.shape[1]
        out[:height, :width] = real.astype(jnp.bfloat16)
        out[:height, width:] = (-imag).astype(jnp.bfloat16)
        out[height:, :width] = imag.astype(jnp.bfloat16)
        out[height:, width:] = real.astype(jnp.bfloat16)

    matrix(first, margin, inner, 0)
    matrix(second, 2 * margin, tile, 1)


def tables(bit_labels, taken, own, slots, tile):
    rows, width = taken.shape[0], own.shape[1]
    inner = rows - 2 * COLS
    vmem, smem = (pl.BlockSpec(memory_space=m) for m in (pltpu.VMEM, pltpu.SMEM))
    return pl.pallas_call(
        functools.partial(tables_kernel, (slots, rows, inner, tile)),
        in_specs=[smem, vmem, vmem],
        out_specs=[smem, vmem, vmem, vmem, vmem],
        out_shape=[
            jax.ShapeDtypeStruct((32,), jnp.int32),
            jax.ShapeDtypeStruct((32, 8, LANES), jnp.float32),
            jax.ShapeDtypeStruct((2 * inner, 2 * width), jnp.bfloat16),
            jax.ShapeDtypeStruct((2 * tile, 2 * width), jnp.bfloat16),
            jax.ShapeDtypeStruct((2, rows, LANES), jnp.float32),
        ],
        compiler_params=pltpu.CompilerParams(vmem_limit_bytes=12 * MEBI),
        cost_estimate=pl.CostEstimate(
            flops=60 * rows * width, bytes_accessed=16 * rows * width, transcendentals=0
        ),
        name="tables",
    )(bit_labels, taken, own)


def on_device(places, element_signals, beam_weights, beam_order, neighbours, leakage, noise_var, bit_labels):
    count = beam_order.shape[0]
    tile = count // places.beam
    rows = tile + 2 * HALO
    slots = neighbours.shape[1]
    width = -(-rows // LANES) * LANES
    padded = jnp.pad(beam_order, (HALO, width + COLS), constant_values=-1)
    group = 2 if places.square else 1
    reach = group * tile
    span = reach + 2 * HALO
    windows = [padded[i : i + count : 1] for i in range(0, span, reach)]
    windows = jnp.concatenate([v.reshape(-1, reach) for v in windows], axis=1)[:, :span]
    own = lax.dynamic_slice_in_dim(padded, lax.axis_index("beam") * tile, width + COLS)
    sides = jnp.stack([own[:width], own[COLS:]]).astype(jnp.float32)
    table = jnp.concatenate(
        [
            neighbours.astype(jnp.float32),
            leakage[0].astype(jnp.float32),
            leakage[1].astype(jnp.float32),
            noise_var[:, None],
        ],
        axis=1,
    )
    taken = jnp.take(table, own[:rows], axis=0, mode="clip")
    held = rows_held(places, beam_weights.shape[1])
    me = lax.axis_index("beam")
    chips = places.beam // 2
    moves = (0, 1, 2, 3)
    if places.square:
        windows = windows[(me // 2) ^ np.array(moves, np.int32)]
    select = (windows[:, :, None] == held[None, None, :]).astype(jnp.bfloat16)
    mine, other = all_beams(places, element_signals, beam_weights, (select, taken, sides))
    beams = [mine]
    if other is not None:
        beams += [places.swap(part, z=1) for part in other]
        taken = after(taken, other[1])
    index, coefs, first, second, scale = tables(bit_labels, taken, sides, slots, tile)
    select = after(select, first, second, scale, coefs)
    ordered = list(order_beams(select, beams))
    elements = element_signals.shape[2] * places.beam
    if places.square:
        here, one, two, three = ordered
        one = places.swap(one, z=1)
        shifts = np.array([0, 0, 1, 2, 1, 2, 3, 3], np.int32)
        flips = np.array([0, 1, 0, 0, 1, 1, 0, 1], np.int32)
        place = me ^ (2 * shifts + flips)
        place = jnp.concatenate([place, (me % 2)[None]])
    else:
        fields = list(
            lax.all_to_all(jnp.stack(ordered), "beam", split_axis=0, concat_axis=0, tiled=True)
        )
        pairs = [fields[2 * i : 2 * i + 2] for i in range(chips)]
        place = jnp.arange(places.beam + 1, dtype=jnp.int32) % places.beam

    def run(turn, pair, before):
        return cancel(turn, place, index, pair, first, second, scale, coefs, elements, before)

    if places.square:
        two = places.swap(two, z=2)
        out = run(0, [here, places.swap(here, core=1)], None)
        one, two = after(one, out), after(two, out)
        three = places.swap(after(three, two), z=3)
        far_one, far_two = places.swap(one, core=1), places.swap(two, core=1)
        out = run(1, [one, two], out)
        out = run(2, [far_one, far_two], out)
        three = after(three, out)
        return run(3, [three, places.swap(three, core=1)], out)
    out = None
    for i in range(chips):
        out = run(i, pairs[i], out)
    return out


def solution(mesh):
    in_specs = (
        P(None, None, ("tm", "beam")),
        P(None, ("tm", "beam"), None),
        P(),
        P(),
        P(),
        P(),
        P(),
    )
    return jax.shard_map(
        functools.partial(on_device, Places(mesh)),
        mesh=mesh,
        in_specs=in_specs,
        out_specs=P(None, "beam", "tm"),
        check_vma=False,
    )
```
